512 devices in a mesh: region: 8 (over z), blk: 64 (over y, x, core).
Axes of the slice: x: 4, y: 8, z: 8, core: 2. Of those that a mesh axis runs over, the one named last changes fastest.
Arguments:
- ensemble: float32 [1024, 256, 128], P(('region', 'blk'))
- observed: float32 [1024, 256, 128], P(('region', 'blk')), may hold values from -6 to 6
- obs_var: float32 [1024, 256], P(('region', 'blk')), may hold values from 0.5 to 2
- ridge: float32 [1024], P(('region', 'blk')), may hold values from 0.05 to 0.5
- pred_back: int32 [1024, 12], P(('region', 'blk')), may hold values from 0 to 16, as said below
- bounds: float32 [2], replicated, may hold values from 0.2 to 6, as said below
Outputs:
- analysis: float32 [1024, 256, 128], P(('region', 'blk'))
The draws below stay inside these ranges and needn't reach their ends.
Inputs may be any that keep to these rules, and one draw needn't show every extreme that they name: `pred_back`: each row holds distinct distances among 1 to 16, never more than the block's own index, with 0 for an empty slot; the last block fills all 12 slots. bounds[0] < bounds[1].
All inputs are finite; a program needn't handle non-finite values.
Results may differ from the reference program's by a relative error of at most 0.0003.
Values sent between devices are 32-bit elements; how exact they have to be, the bound alone decides.
No kernel may reach another device: no remote copies, remote signals or barrier semaphores. Data moves between devices by JAX's collectives and lax.ppermute only.
A program may use at most 192 MiB of HBM per device.

```python
import math
import jax
import jax.numpy as jnp
from jax import lax

M = 128
ROWS = 256
SLOTS = 12
REACH = 16
ITERS = 3
NBLK = 1024


def draw_ensemble(key, part):
    first = jax.random.fold_in(jax.random.fold_in(key, 11), 0)
    noise = jax.random.normal(first, (NBLK, ROWS, M), jnp.float32)

    def advance(carry, fresh):
        state = 0.8 * carry + 0.6 * fresh
        return (state, state)
    start = jnp.zeros((ROWS, M), jnp.float32)
    unused, analysis_output = lax.scan(advance, start, noise)
    return analysis_output


def draw_pred_back(key, part):
    first, second, third = jax.random.split(jax.random.fold_in(key, 23), 3)
    scores = jax.random.randint(first, (NBLK, REACH), 0, 1 << 20) * REACH + jnp.arange(REACH, dtype=jnp.int32)[None, :]
    order = jnp.argsort(scores, axis=1).astype(jnp.int32)
    distance = order[:, :SLOTS] + 1
    base = jax.random.randint(second, (NBLK,), 1, 8)
    many = jax.random.randint(third, (NBLK,), 0, 8) == 0
    blocks = jnp.arange(NBLK, dtype=jnp.int32)
    count = jnp.where(many | (blocks == NBLK - 1), SLOTS, base)
    slot_index = jnp.arange(SLOTS, dtype=jnp.int32)
    chosen = jnp.where(slot_index[None, :] < count[:, None], distance, 0)
    chosen = jnp.where(chosen <= blocks[:, None], chosen, 0)
    return chosen.astype(jnp.int32)


def draw_bounds(key, part):
    first, second = jax.random.split(jax.random.fold_in(key, 37))
    lower_bound = jax.random.uniform(first, (1,), jnp.float32, 0.2, 0.5)
    upper_bound = jax.random.uniform(second, (1,), jnp.float32, 3.0, 6.0)
    return jnp.concatenate([lower_bound, upper_bound])


def shard_levels(stream_key, dims, cuts, smallest, largest):
    gain = 1.0
    for axis_at, parts in cuts:
        heights = jax.random.uniform(jax.random.fold_in(jax.random.fold_in(stream_key, 6), axis_at), (parts,), jnp.float32, smallest / len(cuts), largest / len(cuts))
        gain = gain * jnp.repeat(jnp.exp(heights), dims[axis_at] // parts).reshape((-1,) + (1,) * (len(dims) - 1 - axis_at))
    return gain


def normal_values(rng, extent, spread, bound, cuts=(), held_as=jnp.bfloat16):
    result = spread * jax.random.normal(rng, extent, jnp.float32)
    if cuts:
        result = result * shard_levels(rng, extent, cuts, -0.22, 0.18)
    return jnp.clip(result, -bound, bound).astype(held_as)


def setup_inputs(seed: int = 0) -> dict:
    arg_keys = jax.random.split(jax.random.key(seed), 7)
    ensemble = draw_ensemble(jax.random.fold_in(arg_keys[6], 71), 0)
    observed = normal_values(arg_keys[1], (NBLK, ROWS, M), 1.0, 6.0, ((0, 512),), jnp.float32)
    obs_var = jnp.clip(jnp.exp(math.log(2.0) - 1.3862944 * jax.random.uniform(arg_keys[2], (NBLK, ROWS), jnp.float32) ** shard_levels(arg_keys[2], (NBLK, ROWS), ((0, 512),), -0.2, 0.2)), 0.5, 2.0)
    ridge = jnp.clip(jnp.exp(math.log(0.5) - 2.3025851 * jax.random.uniform(arg_keys[3], (NBLK,), jnp.float32) ** shard_levels(arg_keys[3], (NBLK,), ((0, 512),), -0.2, 0.2)), 0.05, 0.5)
    pred_back = draw_pred_back(jax.random.fold_in(arg_keys[6], 71), 0)
    bounds = draw_bounds(jax.random.fold_in(arg_keys[6], 71), 0)
    return {"ensemble": ensemble, "observed": observed, "obs_var": obs_var, "ridge": ridge, "pred_back": pred_back, "bounds": bounds}


def small_solve(gram, target):
    size = gram.shape[0]
    factor = {}
    for block_position in range(size):
        running = gram[block_position, block_position]
        for k in range(block_position):
            running = running - factor[block_position, k] * factor[block_position, k]
        factor[block_position, block_position] = jnp.sqrt(running)
        for i in range(block_position + 1, size):
            running = gram[i, block_position]
            for k in range(block_position):
                running = running - factor[i, k] * factor[block_position, k]
            factor[i, block_position] = running / factor[block_position, block_position]
    forward = []
    for i in range(size):
        running = target[i]
        for k in range(i):
            running = running - factor[i, k] * forward[k]
        forward.append(running / factor[i, i])
    analysis_output = [None] * size
    for i in reversed(range(size)):
        running = forward[i]
        for k in range(i + 1, size):
            running = running - factor[k, i] * analysis_output[k]
        analysis_output[i] = running / factor[i, i]
    return jnp.stack(analysis_output)

def reference(ensemble, observed, obs_var, ridge, pred_back, bounds):
    highest = lax.Precision.HIGHEST
    nblocks = ensemble.shape[0]
    members = ensemble.shape[2]
    slots = pred_back.shape[1]
    anomaly = (ensemble - lax.optimization_barrier(jnp.mean(ensemble, axis=2, keepdims=True))) / jnp.sqrt(jnp.float32(members - 1))
    empty_zero_matrix = jnp.zeros((1,) + ensemble.shape[1:], ensemble.dtype)
    padded = jnp.concatenate([anomaly, empty_zero_matrix], axis=0)
    block_index_list = jnp.arange(nblocks, dtype=jnp.int32)[:, None] - pred_back
    block_index_list = jnp.where(pred_back > 0, block_index_list, nblocks).astype(jnp.int32)
    identity = jnp.eye(slots, dtype=jnp.float32)

    def regress(inputs):
        own, picked, weight = inputs
        preds = padded[picked]
        gram = jnp.einsum('jrm,krm->jkr', preds, preds, precision=highest) + weight * identity[:, :, None]
        target = jnp.einsum('jrm,rm->jr', preds, own, precision=highest)
        regression_coefficients = small_solve(gram, target)
        resid = own - jnp.einsum('jr,jrm->rm', regression_coefficients, preds, precision=highest)
        return (regression_coefficients, lax.optimization_barrier(jnp.sum(resid * resid, axis=1)) + 1e-05)
    regression_coefficients, dvar = lax.map(regress, (anomaly, block_index_list, ridge))

    def lower(entry_values):
        padded_entry_values = jnp.concatenate([entry_values, empty_zero_matrix], axis=0)
        analysis_output = entry_values
        for block_position in range(slots):
            analysis_output = analysis_output - regression_coefficients[:, block_position, :, None] * padded_entry_values[block_index_list[:, block_position]]
        return analysis_output

    def upper(entry_values):
        analysis_output = jnp.concatenate([entry_values, empty_zero_matrix], axis=0)
        for block_position in range(slots):
            analysis_output = analysis_output.at[block_index_list[:, block_position]].add(-regression_coefficients[:, block_position, :, None] * entry_values)
        return analysis_output[:nblocks]
    inverse_obs = 1.0 / obs_var

    def operator(entry_values):
        return upper(lower(entry_values) / dvar[:, :, None]) + inverse_obs[:, :, None] * entry_values
    lower_bound = bounds[0]
    upper_bound = bounds[1]
    theta = (upper_bound + lower_bound) / 2
    delta = (upper_bound - lower_bound) / 2
    sigma = theta / delta
    rho_now = 1.0 / sigma
    residue = inverse_obs[:, :, None] * (observed - ensemble)
    increment = jnp.zeros_like(ensemble)
    direction = residue / theta
    for step in range(ITERS):
        increment = increment + direction
        residue = residue - operator(direction)
        rho_next = 1.0 / (2 * sigma - rho_now)
        direction = rho_next * rho_now * direction + 2 * rho_next / delta * residue
        rho_now = rho_next
    increment = increment + direction
    return ensemble + increment
```

```python
import jax
import jax.numpy as jnp
from jax import lax
from jax.experimental import pallas as pl
from jax.experimental.pallas import tpu as pltpu
from jax.sharding import PartitionSpec as P

REACH = 16
ITERS = 3
HALO = ITERS * REACH
AXES = ("region", "blk")
LANES = 128
SPAN = 256
CHUNK = 17
META = 16
HIGHEST = lax.Precision.HIGHEST
PARAMS = pltpu.CompilerParams(vmem_limit_bytes=48 * 1024 * 1024)


def iota(shape, axis):
    return lax.broadcasted_iota(jnp.int32, shape, axis)


def pack_kernel(pred_ref, ridge_ref, ens_ref, obs_ref, var_ref, out_ref):
    local_blocks, rows, members = ens_ref.shape
    slots = pred_ref.shape[1]
    last = members - 1
    groups = rows // 8
    low = iota((groups, 8, members), 1) < 4
    lane = iota((rows, members), 1)
    spot = iota((1, members), 1)
    meta = jnp.zeros((1, members), jnp.float32)
    for b in range(local_blocks):
        for k in range(slots):
            meta = jnp.where(spot == META * b + k, pred_ref[b, k].astype(jnp.float32), meta)
        meta = jnp.where(spot == META * b + slots, ridge_ref[b], meta)
        ens = ens_ref[b]
        anomaly = (ens - jnp.mean(ens, axis=1, keepdims=True)) * (1.0 / (members - 1) ** 0.5)
        folded = anomaly + anomaly[:, last:] * (1.0 / (members**0.5 - 1.0))
        variance = jnp.broadcast_to(var_ref[b : b + 1, :], (members, rows)).T
        first = jnp.where(lane == last, variance, folded).reshape(groups, 8, members)
        second = (obs_ref[b] - ens).reshape(groups, 8, members)
        even = jnp.where(low, first, pltpu.roll(second, 4, 1))
        odd = jnp.where(low, pltpu.roll(first, 4, 1), second)
        for q in range(groups):
            at = 2 * q * CHUNK + 8 * b
            out_ref[at : at + 8, :] = even[q]
            out_ref[at + CHUNK : at + CHUNK + 8, :] = odd[q]
    for p in range(2 * groups):
        out_ref[p * CHUNK + CHUNK - 1 : (p + 1) * CHUNK, :] = meta


def add_kernel(ens_ref, inc_ref, out_ref):
    groups, _, _, members = inc_ref.shape
    low = iota((groups, 8, members), 1) < 4
    even, odd = inc_ref[:, 0], inc_ref[:, 1]
    shape = ens_ref.shape[1:]
    out_ref[0] = ens_ref[0] + jnp.where(low, even, pltpu.roll(odd, 4, 1)).reshape(shape)
    out_ref[1] = ens_ref[1] + jnp.where(low, pltpu.roll(even, 4, 1), odd).reshape(shape)


def solve_lags(gram, target):
    size = len(target)
    factor = {}
    inverse = []
    for j in range(size):
        for i in range(j, size):
            running = gram[i, j]
            for k in range(j):
                running = running - factor[i, k] * factor[j, k]
            if i == j:
                inverse.append(lax.rsqrt(running))
            else:
                factor[i, j] = running * inverse[j]
    forward = []
    for i in range(size):
        running = target[i]
        for k in range(i):
            running = running - factor[i, k] * forward[k]
        forward.append(running * inverse[i])
    beta = [None] * size
    for i in reversed(range(size)):
        running = forward[i]
        for k in range(i + 1, size):
            running = running - factor[k, i] * beta[k]
        beta[i] = running * inverse[i]
    return beta


def main_kernel(
    bounds_ref, own_ref, before_ref, after_ref, out_ref,
    tile_ref, x_ref, res_ref, dir_ref, inc_ref, exact_ref, high_ref, low_ref, sums_ref, beta_ref, meta_ref,
):
    rows = 4
    slots = 12
    members = LANES
    sources = [before_ref, own_ref, after_ref]
    counts = [ref.shape[0] // CHUNK for ref in sources]
    blocks = 2 * counts[1]
    chunks = sum(counts)
    at = 0
    for ref, count in zip(sources, counts):
        for s in range(count):
            tile_ref[at : at + 16, :] = ref[s * CHUNK : s * CHUNK + 16, :]
            at += 16
    tile_ref[at:, :] = jnp.zeros((tile_ref.shape[0] - at, members), jnp.float32)

    def column(offset):
        return tile_ref[pl.ds(offset, SPAN, stride=8), :].T

    facts = [ref[pl.ds(CHUNK - 1, count, stride=CHUNK), :] for ref, count in zip(sources, counts)]
    facts = jnp.concatenate(facts + [jnp.zeros((LANES - chunks, members), jnp.float32)], axis=0).T
    spread = iota((LANES, SPAN), 1) - 2 * iota((LANES, SPAN), 0)
    meta_ref[...] = sum(
        jnp.dot(
            facts[META * b : META * (b + 1), :],
            jnp.where(spread == b, 1.0, 0.0),
            precision=HIGHEST,
            preferred_element_type=jnp.float32,
        )
        for b in range(2)
    )

    lower = jnp.full((1, SPAN), bounds_ref[0], jnp.float32)
    higher = jnp.full((1, SPAN), bounds_ref[1], jnp.float32)
    theta = (higher + lower) / 2
    delta = (higher - lower) / 2
    sigma = theta / delta
    rho = 1.0 / sigma
    keep, gain = [], []
    for _ in range(ITERS):
        rho_next = 1.0 / (2 * sigma - rho)
        keep.append(rho_next * rho)
        gain.append(2 * rho_next / delta)
        rho = rho_next

    member = iota((members, SPAN), 0)
    inverse_obs = []
    for r in range(rows):
        x = column(r)
        variance = x[members - 1 :, :]
        inverse_obs.append(1.0 / jnp.where(variance > 0, variance, 1.0))
        x = jnp.where(member == members - 1, 0.0, x)
        x_ref[r] = x
        res_ref[r] = column(4 + r) * inverse_obs[r]
        for lag in range(REACH + 1):
            other = pltpu.roll(x, lag, 1) if lag else x
            total = jnp.sum(x * other, axis=0, keepdims=True)
            sums_ref[lag, r : r + 1, :] = total[:, :LANES]
            sums_ref[lag, 4 + r : 5 + r, :] = total[:, LANES:]

    upper_half = iota((8, LANES), 0) >= 4
    lane = iota((8, LANES), 1)

    def packed(k):
        return jnp.where(upper_half, meta_ref[k : k + 1, LANES:], meta_ref[k : k + 1, :LANES])

    def shifted(value, lag):
        turned = pltpu.roll(value, lag, 1)
        return jnp.where(lane < lag, pltpu.roll(turned, 4, 0), turned)

    picks = [packed(k) for k in range(slots)]
    ridge = packed(slots)
    used = []
    for lag in range(1, REACH + 1):
        hit = jnp.abs(picks[0] - lag) < 0.5
        for k in range(1, slots):
            hit = hit | (jnp.abs(picks[k] - lag) < 0.5)
        used.append(jnp.where(hit, 1.0, 0.0))
    gram = {}
    for i in range(REACH):
        for j in range(i):
            gram[i, j] = shifted(sums_ref[i - j], j + 1) * (used[i] * used[j])
        gram[i, i] = jnp.where(used[i] > 0, shifted(sums_ref[0], i + 1) + ridge, 1.0)
    target = [sums_ref[i + 1] * used[i] for i in range(REACH)]
    beta = solve_lags(gram, target)
    for i in range(REACH):
        beta_ref[i] = -beta[i]

    for half in range(2):
        start = 0 if half == 0 else LANES - REACH
        stop = LANES * (half + 1)
        shape = (stop - start, LANES)
        lag_of = iota(shape, 1) + half * LANES - iota(shape, 0) - start
        lanes = slice(half * LANES, (half + 1) * LANES)
        for r in range(rows):
            factor = jnp.where(lag_of == 0, 1.0, 0.0)
            for lag in range(1, REACH + 1):
                value = beta_ref[lag - 1, 4 * half + r : 4 * half + r + 1, :]
                factor = jnp.where(lag_of == lag, value, factor)
            high = factor.astype(jnp.bfloat16)
            exact_ref[r, start:stop, lanes] = factor
            high_ref[r, start:stop, lanes] = high
            low_ref[r, start:stop, lanes] = (factor - high.astype(jnp.float32)).astype(jnp.bfloat16)
            rest = slice(stop, SPAN) if half == 0 else slice(0, start)
            empty = (rest.stop - rest.start, LANES)
            exact_ref[r, rest, lanes] = jnp.zeros(empty, jnp.float32)
            high_ref[r, rest, lanes] = jnp.zeros(empty, jnp.bfloat16)
            low_ref[r, rest, lanes] = jnp.zeros(empty, jnp.bfloat16)

    inverse_var = []
    for r in range(rows):
        resid = jnp.dot(
            x_ref[r], exact_ref[r], precision=HIGHEST, preferred_element_type=jnp.float32
        )
        inverse_var.append(1.0 / (jnp.sum(resid * resid, axis=0, keepdims=True) + 1e-05))

    def product(value, r, axis):
        high = value.astype(jnp.bfloat16)
        low = (value - high.astype(jnp.float32)).astype(jnp.bfloat16)
        dims = (((1,), (axis,)), ((), ()))

        def dot(a, b):
            return lax.dot_general(a, b, dims, preferred_element_type=jnp.float32)

        return dot(high, high_ref[r]) + (dot(low, high_ref[r]) + dot(high, low_ref[r]))

    for r in range(rows):
        dir_ref[r] = res_ref[r] / theta
        inc_ref[r] = dir_ref[r]
    for step in range(ITERS):
        for r in range(rows):
            direction = dir_ref[r]
            middle = product(direction, r, 0) * inverse_var[r]
            residue = res_ref[r] - (product(middle, r, 1) + inverse_obs[r] * direction)
            direction = keep[step] * direction + gain[step] * residue
            res_ref[r] = residue
            dir_ref[r] = direction
            inc_ref[r] = inc_ref[r] + direction
    for r in range(rows):
        own = pltpu.roll(inc_ref[r], SPAN - HALO, 1)[:, :blocks]
        out_ref[pl.ds(r, blocks, stride=4), :] = own.T


def vmem(count):
    return [pl.BlockSpec(memory_space=pltpu.VMEM)] * count


def run_main(bounds, own, before, after):
    members, per_device = own.shape[1], 4
    blocks = own.shape[0] // CHUNK * 2
    return pl.pallas_call(
        main_kernel,
        out_shape=jax.ShapeDtypeStruct((blocks * per_device, members), jnp.float32),
        in_specs=[pl.BlockSpec(memory_space=pltpu.SMEM)] + vmem(3),
        out_specs=vmem(1)[0],
        scratch_shapes=[pltpu.VMEM((8 * SPAN, members), jnp.float32)]
        + [pltpu.VMEM((per_device, members, SPAN), jnp.float32)] * 4
        + [
            pltpu.VMEM((per_device, SPAN, SPAN), jnp.float32),
            pltpu.VMEM((per_device, SPAN, SPAN), jnp.bfloat16),
            pltpu.VMEM((per_device, SPAN, SPAN), jnp.bfloat16),
            pltpu.VMEM((REACH + 1, 8, LANES), jnp.float32),
            pltpu.VMEM((REACH, 8, LANES), jnp.float32),
            pltpu.VMEM((META, SPAN), jnp.float32),
        ],
        compiler_params=PARAMS,
        name="solve",
    )(bounds, own, before, after)


def on_device(ensemble, observed, obs_var, ridge, pred_back, bounds):
    local_blocks, rows, members = ensemble.shape
    slots = pred_back.shape[1]
    region_blocks = lax.axis_size("blk") * local_blocks
    regions = lax.axis_size("region")
    per_device = rows // lax.axis_size("blk")
    assert (local_blocks, per_device, members, region_blocks) == (2, 4, LANES, LANES)
    groups = rows // 8
    peers = 2 * groups
    packed = pl.pallas_call(
        pack_kernel,
        out_shape=jax.ShapeDtypeStruct((peers * CHUNK, members), jnp.float32),
        in_specs=[pl.BlockSpec(memory_space=pltpu.SMEM)] * 2 + vmem(3),
        out_specs=vmem(1)[0],
        compiler_params=PARAMS,
        name="pack",
    )(pred_back, ridge, ensemble, observed, obs_var)
    own = lax.all_to_all(packed.reshape(peers, 1, CHUNK * members), "blk", 0, 0, tiled=True)
    own = own.reshape(peers * CHUNK, members)
    up = [(i, i + 1) for i in range(regions - 1)]
    edge = HALO // local_blocks * CHUNK
    before = lax.ppermute(own[own.shape[0] - edge :], "region", up)
    after = lax.ppermute(own[:edge], "region", [(b, a) for a, b in up])
    increment = run_main(bounds, own, before, after)
    increment = increment.reshape(2 * groups, local_blocks * per_device, members)
    increment = lax.all_to_all(increment, "blk", 0, 0, tiled=True)
    return pl.pallas_call(
        add_kernel,
        out_shape=jax.ShapeDtypeStruct(ensemble.shape, jnp.float32),
        in_specs=vmem(2),
        out_specs=vmem(1)[0],
        compiler_params=PARAMS,
        name="add",
    )(ensemble, increment.reshape(groups, 2, 8, members))


def solution(mesh):
    return jax.shard_map(
        on_device,
        mesh=mesh,
        in_specs=(
            P(AXES, None, None),
            P(AXES, None, None),
            P(AXES, None),
            P(AXES),
            P(AXES, None),
            P(),
        ),
        out_specs=P(AXES, None, None),
        check_vma=False,
    )
```

```python
import jax
import jax.numpy as jnp
from jax import lax
from jax.experimental import pallas as pl
from jax.experimental.pallas import tpu as pltpu
from jax.sharding import PartitionSpec as P

REACH = 16
ITERS = 3
HALO = ITERS * REACH
AXES = ("region", "blk")
LANES = 128
SPAN = 256
FIRST = 9
SECOND = 8
CHUNK = FIRST + SECOND
META = 16
HIGHEST = lax.Precision.HIGHEST
PARAMS = pltpu.CompilerParams(vmem_limit_bytes=48 * 1024 * 1024)


def iota(shape, axis):
    return lax.broadcasted_iota(jnp.int32, shape, axis)


def pack_kernel(
    pred_hbm, ridge_hbm, ens_hbm, obs_hbm, var_hbm, out_ref,
    pred_ref, ridge_ref, ens_ref, obs_ref, var_ref, sems,
):
    pairs = [
        (ens_hbm, ens_ref), (var_hbm, var_ref), (pred_hbm, pred_ref), (ridge_hbm, ridge_ref),
        (obs_hbm, obs_ref),
    ]
    copies = [pltpu.make_async_copy(a, b, sems.at[i]) for i, (a, b) in enumerate(pairs)]
    for copy in copies:
        copy.start()
    local_blocks, rows, members = ens_ref.shape
    slots = pred_ref.shape[1]
    last = members - 1
    groups = rows // 8
    low = iota((groups, 8, members), 1) < 4
    lane = iota((rows, members), 1)
    spot = iota((1, members), 1)

    def deal(blocks, start):
        blocks = [block.reshape(groups, 8, members) for block in blocks]
        even = jnp.where(low, blocks[0], pltpu.roll(blocks[1], 4, 1))
        odd = jnp.where(low, pltpu.roll(blocks[0], 4, 1), blocks[1])
        for q in range(groups):
            at = 2 * q * CHUNK + start
            out_ref[at : at + 8, :] = even[q]
            out_ref[at + CHUNK : at + CHUNK + 8, :] = odd[q]

    for copy in copies[:4]:
        copy.wait()
    meta = jnp.zeros((1, members), jnp.float32)
    blocks = []
    for b in range(local_blocks):
        for k in range(slots):
            meta = jnp.where(spot == META * b + k, pred_ref[b, k].astype(jnp.float32), meta)
        meta = jnp.where(spot == META * b + slots, ridge_ref[b], meta)
        ens = ens_ref[b]
        anomaly = (ens - jnp.mean(ens, axis=1, keepdims=True)) * (1.0 / (members - 1) ** 0.5)
        folded = anomaly + anomaly[:, last:] * (1.0 / (members**0.5 - 1.0))
        variance = jnp.broadcast_to(var_ref[b : b + 1, :], (members, rows)).T
        blocks.append(jnp.where(lane == last, variance, folded))
    deal(blocks, 0)
    for p in range(2 * groups):
        out_ref[p * CHUNK + FIRST - 1 : p * CHUNK + FIRST, :] = meta
    copies[4].wait()
    deal([obs_ref[b] - ens_ref[b] for b in range(local_blocks)], FIRST)


def add_kernel(ens_ref, inc_ref, out_ref):
    groups, _, _, members = inc_ref.shape
    low = iota((groups, 8, members), 1) < 4
    even, odd = inc_ref[:, 0], inc_ref[:, 1]
    shape = ens_ref.shape[1:]
    out_ref[0] = ens_ref[0] + jnp.where(low, even, pltpu.roll(odd, 4, 1)).reshape(shape)
    out_ref[1] = ens_ref[1] + jnp.where(low, pltpu.roll(even, 4, 1), odd).reshape(shape)


def solve_lags(gram, target):
    size = len(target)
    factor = {}
    inverse = []
    for j in range(size):
        for i in range(j, size):
            running = gram[i, j]
            for k in range(j):
                running = running - factor[i, k] * factor[j, k]
            if i == j:
                inverse.append(lax.rsqrt(running))
            else:
                factor[i, j] = running * inverse[j]
    forward = []
    for i in range(size):
        running = target[i]
        for k in range(i):
            running = running - factor[i, k] * forward[k]
        forward.append(running * inverse[i])
    beta = [None] * size
    for i in reversed(range(size)):
        running = forward[i]
        for k in range(i + 1, size):
            running = running - factor[k, i] * beta[k]
        beta[i] = running * inverse[i]
    return beta


def line_up(sources, tile_ref):
    at = 0
    for ref, stride, start in sources:
        for s in range(start, ref.shape[0], stride):
            tile_ref[at : at + 8, :] = ref[s : s + 8, :]
            at += 8
    tile_ref[at:, :] = jnp.zeros((tile_ref.shape[0] - at, tile_ref.shape[1]), jnp.float32)


def regress_kernel(
    own_ref, before_ref, after_ref, high_ref, low_ref, inverse_ref,
    tile_ref, x_ref, exact_ref, sums_ref, beta_ref, meta_ref,
):
    rows = 4
    slots = 12
    members = LANES
    sources = [(before_ref, FIRST, 0), (own_ref, CHUNK, 0), (after_ref, FIRST, 0)]
    line_up(sources, tile_ref)

    facts = [ref[pl.ds(FIRST - 1, ref.shape[0] // n, stride=n), :] for ref, n, _ in sources]
    chunks = sum(len(fact) for fact in facts)
    facts = jnp.concatenate(facts + [jnp.zeros((LANES - chunks, members), jnp.float32)], axis=0).T
    spread = iota((LANES, SPAN), 1) - 2 * iota((LANES, SPAN), 0)
    meta_ref[...] = sum(
        jnp.dot(
            facts[META * b : META * (b + 1), :],
            jnp.where(spread == b, 1.0, 0.0),
            precision=HIGHEST,
            preferred_element_type=jnp.float32,
        )
        for b in range(2)
    )

    member = iota((members, SPAN), 0)
    for r in range(rows):
        x = tile_ref[pl.ds(r, SPAN, stride=4), :].T
        variance = x[members - 1 :, :]
        inverse_ref[4 + r : 5 + r, :] = 1.0 / jnp.where(variance > 0, variance, 1.0)
        x = jnp.where(member == members - 1, 0.0, x)
        x_ref[r] = x
        for lag in range(REACH + 1):
            other = pltpu.roll(x, lag, 1) if lag else x
            total = jnp.sum(x * other, axis=0, keepdims=True)
            sums_ref[lag, r : r + 1, :] = total[:, :LANES]
            sums_ref[lag, 4 + r : 5 + r, :] = total[:, LANES:]

    upper_half = iota((8, LANES), 0) >= 4
    lane = iota((8, LANES), 1)

    def packed(k):
        return jnp.where(upper_half, meta_ref[k : k + 1, LANES:], meta_ref[k : k + 1, :LANES])

    def shifted(value, lag):
        turned = pltpu.roll(value, lag, 1)
        return jnp.where(lane < lag, pltpu.roll(turned, 4, 0), turned)

    picks = [packed(k) for k in range(slots)]
    ridge = packed(slots)
    used = []
    for lag in range(1, REACH + 1):
        hit = jnp.abs(picks[0] - lag) < 0.5
        for k in range(1, slots):
            hit = hit | (jnp.abs(picks[k] - lag) < 0.5)
        used.append(jnp.where(hit, 1.0, 0.0))
    gram = {}
    for i in range(REACH):
        for j in range(i):
            gram[i, j] = shifted(sums_ref[i - j], j + 1) * (used[i] * used[j])
        gram[i, i] = jnp.where(used[i] > 0, shifted(sums_ref[0], i + 1) + ridge, 1.0)
    target = [sums_ref[i + 1] * used[i] for i in range(REACH)]
    beta = solve_lags(gram, target)
    for i in range(REACH):
        beta_ref[i] = -beta[i]

    for half in range(2):
        start = 0 if half == 0 else LANES - REACH
        stop = LANES * (half + 1)
        shape = (stop - start, LANES)
        lag_of = iota(shape, 1) + half * LANES - iota(shape, 0) - start
        lanes = slice(half * LANES, (half + 1) * LANES)
        for r in range(rows):
            factor = jnp.where(lag_of == 0, 1.0, 0.0)
            for lag in range(1, REACH + 1):
                value = beta_ref[lag - 1, 4 * half + r : 4 * half + r + 1, :]
                factor = jnp.where(lag_of == lag, value, factor)
            high = factor.astype(jnp.bfloat16)
            exact_ref[r, start:stop, lanes] = factor
            high_ref[r, start:stop, lanes] = high
            low_ref[r, start:stop, lanes] = (factor - high.astype(jnp.float32)).astype(jnp.bfloat16)
            rest = slice(stop, SPAN) if half == 0 else slice(0, start)
            empty = (rest.stop - rest.start, LANES)
            exact_ref[r, rest, lanes] = jnp.zeros(empty, jnp.float32)
            high_ref[r, rest, lanes] = jnp.zeros(empty, jnp.bfloat16)
            low_ref[r, rest, lanes] = jnp.zeros(empty, jnp.bfloat16)

    for r in range(rows):
        resid = jnp.dot(
            x_ref[r], exact_ref[r], precision=HIGHEST, preferred_element_type=jnp.float32
        )
        total = jnp.sum(resid * resid, axis=0, keepdims=True)
        inverse_ref[r : r + 1, :] = 1.0 / (total + 1e-05)


def iterate_kernel(
    bounds_hbm, own_ref, before_ref, after_ref, high_ref, low_ref, inverse_ref, out_ref,
    tile_ref, res_ref, dir_ref, inc_ref, bounds_ref, sem,
):
    rows = 4
    members = LANES
    blocks = out_ref.shape[0] // rows
    copy = pltpu.make_async_copy(bounds_hbm, bounds_ref, sem)
    copy.start()
    line_up([(before_ref, SECOND, 0), (own_ref, CHUNK, FIRST), (after_ref, SECOND, 0)], tile_ref)
    copy.wait()
    lower = jnp.full((1, SPAN), bounds_ref[0], jnp.float32)
    higher = jnp.full((1, SPAN), bounds_ref[1], jnp.float32)
    theta = (higher + lower) / 2
    delta = (higher - lower) / 2
    sigma = theta / delta
    rho = 1.0 / sigma

    def product(value, r, axis):
        high = value.astype(jnp.bfloat16)
        low = (value - high.astype(jnp.float32)).astype(jnp.bfloat16)
        dims = (((1,), (axis,)), ((), ()))

        def dot(a, b):
            return lax.dot_general(a, b, dims, preferred_element_type=jnp.float32)

        both = dot(jnp.concatenate([high, low], axis=0), high_ref[r])
        return both[:members] + (both[members:] + dot(high, low_ref[r]))

    for r in range(rows):
        residue = tile_ref[pl.ds(r, SPAN, stride=rows), :].T * inverse_ref[4 + r : 5 + r, :]
        res_ref[r] = residue
        dir_ref[r] = residue / theta
        inc_ref[r] = dir_ref[r]
    for _ in range(ITERS):
        rho_next = 1.0 / (2 * sigma - rho)
        for r in range(rows):
            direction = dir_ref[r]
            middle = product(direction, r, 0) * inverse_ref[r : r + 1, :]
            applied = product(middle, r, 1) + inverse_ref[4 + r : 5 + r, :] * direction
            residue = res_ref[r] - applied
            direction = (rho_next * rho) * direction + (2 * rho_next / delta) * residue
            res_ref[r] = residue
            dir_ref[r] = direction
            inc_ref[r] = inc_ref[r] + direction
        rho = rho_next
    for r in range(rows):
        own = pltpu.roll(inc_ref[r], SPAN - HALO, 1)[:, :blocks]
        out_ref[pl.ds(r, blocks, stride=rows), :] = own.T


def vmem(count):
    return [pl.BlockSpec(memory_space=pltpu.VMEM)] * count


def hbm(count):
    return [pl.BlockSpec(memory_space=pltpu.HBM)] * count


def pack(pred_back, ridge, ensemble, observed, obs_var):
    local_blocks, rows, members = ensemble.shape
    peers = rows // 4
    operands = [
        pltpu.with_memory_space_constraint(value, pltpu.HBM)
        for value in (pred_back, ridge, ensemble, observed, obs_var)
    ]
    return pl.pallas_call(
        pack_kernel,
        out_shape=jax.ShapeDtypeStruct((peers * CHUNK, members), jnp.float32),
        in_specs=hbm(5),
        out_specs=vmem(1)[0],
        scratch_shapes=[
            pltpu.SMEM(pred_back.shape, jnp.int32),
            pltpu.SMEM(ridge.shape, jnp.float32),
            pltpu.VMEM(ensemble.shape, jnp.float32),
            pltpu.VMEM(observed.shape, jnp.float32),
            pltpu.VMEM(obs_var.shape, jnp.float32),
            pltpu.SemaphoreType.DMA((5,)),
        ],
        compiler_params=PARAMS,
        name="pack",
    )(*operands)


def regress(own, before, after):
    members, rows = own.shape[1], 4
    square = (rows, SPAN, SPAN)
    return pl.pallas_call(
        regress_kernel,
        out_shape=[
            jax.ShapeDtypeStruct(square, jnp.bfloat16),
            jax.ShapeDtypeStruct(square, jnp.bfloat16),
            jax.ShapeDtypeStruct((8, SPAN), jnp.float32),
        ],
        in_specs=vmem(3),
        out_specs=vmem(3),
        scratch_shapes=[
            pltpu.VMEM((4 * SPAN, members), jnp.float32),
            pltpu.VMEM((rows, members, SPAN), jnp.float32),
            pltpu.VMEM(square, jnp.float32),
            pltpu.VMEM((REACH + 1, 8, LANES), jnp.float32),
            pltpu.VMEM((REACH, 8, LANES), jnp.float32),
            pltpu.VMEM((META, SPAN), jnp.float32),
        ],
        compiler_params=PARAMS,
        name="regress",
    )(own, before, after)


def iterate(bounds, own, before, after, factors):
    members, rows = own.shape[1], 4
    return pl.pallas_call(
        iterate_kernel,
        out_shape=jax.ShapeDtypeStruct((own.shape[0] // CHUNK * 2 * rows, members), jnp.float32),
        in_specs=hbm(1) + vmem(6),
        out_specs=vmem(1)[0],
        scratch_shapes=[pltpu.VMEM((4 * SPAN, members), jnp.float32)]
        + [pltpu.VMEM((rows, members, SPAN), jnp.float32)] * 3
        + [pltpu.SMEM(bounds.shape, jnp.float32), pltpu.SemaphoreType.DMA],
        compiler_params=PARAMS,
        name="iterate",
    )(pltpu.with_memory_space_constraint(bounds, pltpu.HBM), own, before, after, *factors)


def on_device(ensemble, observed, obs_var, ridge, pred_back, bounds):
    local_blocks, rows, members = ensemble.shape
    slots = pred_back.shape[1]
    region_blocks = lax.axis_size("blk") * local_blocks
    regions = lax.axis_size("region")
    per_device = rows // lax.axis_size("blk")
    assert (local_blocks, per_device, members, region_blocks) == (2, 4, LANES, LANES)
    groups = rows // 8
    peers = 2 * groups
    up = [(i, i + 1) for i in range(regions - 1)]
    down = [(b, a) for a, b in up]

    packed = pack(pred_back, ridge, ensemble, observed, obs_var)
    own = lax.all_to_all(packed.reshape(peers, 1, CHUNK * members), "blk", 0, 0, tiled=True)
    edge = HALO // local_blocks

    def halo(start, rows):
        part = own[:, :, start * members : (start + rows) * members]
        pieces = [lax.ppermute(part[peers - edge :], "region", up), lax.ppermute(part[:edge], "region", down)]
        return [piece.reshape(edge * rows, members) for piece in pieces]

    first, second = halo(0, FIRST), halo(FIRST, SECOND)
    own = own.reshape(peers * CHUNK, members)
    increment = iterate(bounds, own, *second, regress(own, *first))
    increment = increment.reshape(2 * groups, local_blocks * per_device, members)
    increment = lax.all_to_all(increment, "blk", 0, 0, tiled=True)
    return pl.pallas_call(
        add_kernel,
        out_shape=jax.ShapeDtypeStruct(ensemble.shape, jnp.float32),
        in_specs=vmem(2),
        out_specs=vmem(1)[0],
        compiler_params=PARAMS,
        name="add",
    )(ensemble, increment.reshape(groups, 2, 8, members))


def solution(mesh):
    return jax.shard_map(
        on_device,
        mesh=mesh,
        in_specs=(
            P(AXES, None, None),
            P(AXES, None, None),
            P(AXES, None),
            P(AXES),
            P(AXES, None),
            P(),
        ),
        out_specs=P(AXES, None, None),
        check_vma=False,
    )
```

```python
import jax
import jax.numpy as jnp
from jax import lax
from jax.experimental import pallas as pl
from jax.experimental.pallas import tpu as pltpu
from jax.sharding import PartitionSpec as P

REACH = 16
ITERS = 3
HALO = ITERS * REACH
AXES = ("region", "blk")
LANES = 128
SPAN = 256
FIRST = 9
SECOND = 8
CHUNK = FIRST + SECOND
META = 16
HIGHEST = lax.Precision.HIGHEST
PARAMS = pltpu.CompilerParams(vmem_limit_bytes=48 * 1024 * 1024)


def iota(shape, axis):
    return lax.broadcasted_iota(jnp.int32, shape, axis)


def pack_kernel(
    pred_hbm, ridge_hbm, ens_hbm, obs_hbm, var_hbm, out_ref,
    pred_ref, ridge_ref, ens_ref, obs_ref, var_ref, sems,
):
    pairs = [
        (ens_hbm, ens_ref), (var_hbm, var_ref), (pred_hbm, pred_ref), (ridge_hbm, ridge_ref),
        (obs_hbm, obs_ref),
    ]
    copies = [pltpu.make_async_copy(a, b, sems.at[i]) for i, (a, b) in enumerate(pairs)]
    for copy in copies:
        copy.start()
    local_blocks, rows, members = ens_ref.shape
    slots = pred_ref.shape[1]
    last = members - 1
    groups = rows // 8
    low = iota((groups, 8, members), 1) < 4
    lane = iota((rows, members), 1)
    spot = iota((1, members), 1)

    def deal(blocks, start):
        blocks = [block.reshape(groups, 8, members) for block in blocks]
        even = jnp.where(low, blocks[0], pltpu.roll(blocks[1], 4, 1))
        odd = jnp.where(low, pltpu.roll(blocks[0], 4, 1), blocks[1])
        for q in range(groups):
            at = 2 * q * CHUNK + start
            out_ref[at : at + 8, :] = even[q]
            out_ref[at + CHUNK : at + CHUNK + 8, :] = odd[q]

    for copy in copies[:4]:
        copy.wait()
    meta = jnp.zeros((1, members), jnp.float32)
    blocks = []
    for b in range(local_blocks):
        for k in range(slots):
            meta = jnp.where(spot == META * b + k, pred_ref[b, k].astype(jnp.float32), meta)
        meta = jnp.where(spot == META * b + slots, ridge_ref[b], meta)
        ens = ens_ref[b]
        anomaly = (ens - jnp.mean(ens, axis=1, keepdims=True)) * (1.0 / (members - 1) ** 0.5)
        folded = anomaly + anomaly[:, last:] * (1.0 / (members**0.5 - 1.0))
        variance = jnp.broadcast_to(var_ref[b : b + 1, :], (members, rows)).T
        blocks.append(jnp.where(lane == last, variance, folded))
    deal(blocks, 0)
    for p in range(2 * groups):
        out_ref[p * CHUNK + FIRST - 1 : p * CHUNK + FIRST, :] = meta
    copies[4].wait()
    deal([obs_ref[b] - ens_ref[b] for b in range(local_blocks)], FIRST)


def add_kernel(ens_ref, inc_ref, out_ref):
    groups, _, _, members = inc_ref.shape
    low = iota((groups, 8, members), 1) < 4
    even, odd = inc_ref[:, 0], inc_ref[:, 1]
    shape = ens_ref.shape[1:]
    out_ref[0] = ens_ref[0] + jnp.where(low, even, pltpu.roll(odd, 4, 1)).reshape(shape)
    out_ref[1] = ens_ref[1] + jnp.where(low, pltpu.roll(even, 4, 1), odd).reshape(shape)


def solve_lags(gram, target):
    size = len(target)
    factor = {}
    inverse = []
    for j in range(size):
        for i in range(j, size):
            running = gram[i, j]
            for k in range(j):
                running = running - factor[i, k] * factor[j, k]
            if i == j:
                inverse.append(lax.rsqrt(running))
            else:
                factor[i, j] = running * inverse[j]
    forward = []
    for i in range(size):
        running = target[i]
        for k in range(i):
            running = running - factor[i, k] * forward[k]
        forward.append(running * inverse[i])
    beta = [None] * size
    for i in reversed(range(size)):
        running = forward[i]
        for k in range(i + 1, size):
            running = running - factor[k, i] * beta[k]
        beta[i] = running * inverse[i]
    return beta


def parity():
    return lax.axis_index("blk") % 2


def solve_kernel(
    bounds_hbm, own_ref, first_ref, second_ref, out_ref,
    tile_ref, fact_ref, x_ref, exact_ref, high_ref, low_ref, inverse_ref,
    sums_ref, beta_ref, meta_ref, res_ref, dir_ref, inc_ref, bounds_ref, sem,
):
    copy = pltpu.make_async_copy(bounds_hbm, bounds_ref, sem)
    copy.start()
    edge = first_ref.shape[0] // CHUNK
    peers = own_ref.shape[0] // CHUNK

    def line_up(ref, at):
        count = ref.shape[0] // CHUNK
        for s in range(count):
            for part, start in enumerate((0, FIRST)):
                row = s * CHUNK + start
                tile_ref[part, 8 * (at + s) : 8 * (at + s + 1), :] = ref[row : row + 8, :]
        fact_ref[at : at + count, :] = ref[pl.ds(FIRST - 1, count, stride=CHUNK), :]

    end = 2 * edge + peers
    tile_ref[:, 8 * end :, :] = jnp.zeros((2, tile_ref.shape[1] - 8 * end, LANES), jnp.float32)
    fact_ref[end:, :] = jnp.zeros((LANES - end, LANES), jnp.float32)
    line_up(own_ref, edge)
    for turn in range(2):

        @pl.when(parity() == turn)
        def _():
            line_up((first_ref, second_ref)[turn], 0)
            line_up((second_ref, first_ref)[turn], edge + peers)

    regress(
        tile_ref.at[0], fact_ref, high_ref, low_ref, inverse_ref,
        x_ref, exact_ref, sums_ref, beta_ref, meta_ref,
    )
    copy.wait()
    iterate(
        bounds_ref, tile_ref.at[1], high_ref, low_ref, inverse_ref, out_ref, res_ref, dir_ref, inc_ref
    )


def regress(
    tile_ref, fact_ref, high_ref, low_ref, inverse_ref, x_ref, exact_ref, sums_ref, beta_ref, meta_ref
):
    rows = 4
    slots = 12
    members = LANES
    facts = fact_ref[...].T
    spread = iota((LANES, SPAN), 1) - 2 * iota((LANES, SPAN), 0)
    meta_ref[...] = sum(
        jnp.dot(
            facts[META * b : META * (b + 1), :],
            jnp.where(spread == b, 1.0, 0.0),
            precision=HIGHEST,
            preferred_element_type=jnp.float32,
        )
        for b in range(2)
    )

    member = iota((members, SPAN), 0)
    for r in range(rows):
        x = tile_ref[pl.ds(r, SPAN, stride=4), :].T
        variance = x[members - 1 :, :]
        inverse_ref[4 + r : 5 + r, :] = 1.0 / jnp.where(variance > 0, variance, 1.0)
        x = jnp.where(member == members - 1, 0.0, x)
        x_ref[r] = x
        for lag in range(REACH + 1):
            other = pltpu.roll(x, lag, 1) if lag else x
            total = jnp.sum(x * other, axis=0, keepdims=True)
            sums_ref[lag, r : r + 1, :] = total[:, :LANES]
            sums_ref[lag, 4 + r : 5 + r, :] = total[:, LANES:]

    upper_half = iota((8, LANES), 0) >= 4
    lane = iota((8, LANES), 1)

    def packed(k):
        return jnp.where(upper_half, meta_ref[k : k + 1, LANES:], meta_ref[k : k + 1, :LANES])

    def shifted(value, lag):
        turned = pltpu.roll(value, lag, 1)
        return jnp.where(lane < lag, pltpu.roll(turned, 4, 0), turned)

    picks = [packed(k) for k in range(slots)]
    ridge = packed(slots)
    used = []
    for lag in range(1, REACH + 1):
        hit = jnp.abs(picks[0] - lag) < 0.5
        for k in range(1, slots):
            hit = hit | (jnp.abs(picks[k] - lag) < 0.5)
        used.append(jnp.where(hit, 1.0, 0.0))
    gram = {}
    for i in range(REACH):
        for j in range(i):
            gram[i, j] = shifted(sums_ref[i - j], j + 1) * (used[i] * used[j])
        gram[i, i] = jnp.where(used[i] > 0, shifted(sums_ref[0], i + 1) + ridge, 1.0)
    target = [sums_ref[i + 1] * used[i] for i in range(REACH)]
    beta = solve_lags(gram, target)
    for i in range(REACH):
        beta_ref[i] = -beta[i]

    for half in range(2):
        start = 0 if half == 0 else LANES - REACH
        stop = LANES * (half + 1)
        shape = (stop - start, LANES)
        lag_of = iota(shape, 1) + half * LANES - iota(shape, 0) - start
        lanes = slice(half * LANES, (half + 1) * LANES)
        for r in range(rows):
            factor = jnp.where(lag_of == 0, 1.0, 0.0)
            for lag in range(1, REACH + 1):
                value = beta_ref[lag - 1, 4 * half + r : 4 * half + r + 1, :]
                factor = jnp.where(lag_of == lag, value, factor)
            high = factor.astype(jnp.bfloat16)
            exact_ref[r, start:stop, lanes] = factor
            high_ref[r, start:stop, lanes] = high
            low_ref[r, start:stop, lanes] = (factor - high.astype(jnp.float32)).astype(jnp.bfloat16)
            rest = slice(stop, SPAN) if half == 0 else slice(0, start)
            empty = (rest.stop - rest.start, LANES)
            exact_ref[r, rest, lanes] = jnp.zeros(empty, jnp.float32)
            high_ref[r, rest, lanes] = jnp.zeros(empty, jnp.bfloat16)
            low_ref[r, rest, lanes] = jnp.zeros(empty, jnp.bfloat16)

    for r in range(rows):
        resid = jnp.dot(
            x_ref[r], exact_ref[r], precision=HIGHEST, preferred_element_type=jnp.float32
        )
        total = jnp.sum(resid * resid, axis=0, keepdims=True)
        inverse_ref[r : r + 1, :] = 1.0 / (total + 1e-05)


def iterate(bounds_ref, tile_ref, high_ref, low_ref, inverse_ref, out_ref, res_ref, dir_ref, inc_ref):
    rows = 4
    members = LANES
    blocks = out_ref.shape[0] // rows
    lower = jnp.full((1, SPAN), bounds_ref[0], jnp.float32)
    higher = jnp.full((1, SPAN), bounds_ref[1], jnp.float32)
    theta = (higher + lower) / 2
    delta = (higher - lower) / 2
    sigma = theta / delta
    rho = 1.0 / sigma

    def product(value, r, axis):
        high = value.astype(jnp.bfloat16)
        low = (value - high.astype(jnp.float32)).astype(jnp.bfloat16)
        dims = (((1,), (axis,)), ((), ()))

        def dot(a, b):
            return lax.dot_general(a, b, dims, preferred_element_type=jnp.float32)

        both = dot(jnp.concatenate([high, low], axis=0), high_ref[r])
        return both[:members] + (both[members:] + dot(high, low_ref[r]))

    for r in range(rows):
        residue = tile_ref[pl.ds(r, SPAN, stride=rows), :].T * inverse_ref[4 + r : 5 + r, :]
        res_ref[r] = residue
        dir_ref[r] = residue / theta
        inc_ref[r] = dir_ref[r]
    for _ in range(ITERS):
        rho_next = 1.0 / (2 * sigma - rho)
        for r in range(rows):
            direction = dir_ref[r]
            middle = product(direction, r, 0) * inverse_ref[r : r + 1, :]
            applied = product(middle, r, 1) + inverse_ref[4 + r : 5 + r, :] * direction
            residue = res_ref[r] - applied
            direction = (rho_next * rho) * direction + (2 * rho_next / delta) * residue
            res_ref[r] = residue
            dir_ref[r] = direction
            inc_ref[r] = inc_ref[r] + direction
        rho = rho_next
    for r in range(rows):
        own = pltpu.roll(inc_ref[r], SPAN - HALO, 1)[:, :blocks]
        out_ref[pl.ds(r, blocks, stride=rows), :] = own.T


def vmem(count):
    return [pl.BlockSpec(memory_space=pltpu.VMEM)] * count


def hbm(count):
    return [pl.BlockSpec(memory_space=pltpu.HBM)] * count


def pack(pred_back, ridge, ensemble, observed, obs_var):
    local_blocks, rows, members = ensemble.shape
    peers = rows // 4
    operands = [
        pltpu.with_memory_space_constraint(value, pltpu.HBM)
        for value in (pred_back, ridge, ensemble, observed, obs_var)
    ]
    return pl.pallas_call(
        pack_kernel,
        out_shape=jax.ShapeDtypeStruct((peers * CHUNK, members), jnp.float32),
        in_specs=hbm(5),
        out_specs=vmem(1)[0],
        scratch_shapes=[
            pltpu.SMEM(pred_back.shape, jnp.int32),
            pltpu.SMEM(ridge.shape, jnp.float32),
            pltpu.VMEM(ensemble.shape, jnp.float32),
            pltpu.VMEM(observed.shape, jnp.float32),
            pltpu.VMEM(obs_var.shape, jnp.float32),
            pltpu.SemaphoreType.DMA((5,)),
        ],
        compiler_params=PARAMS,
        name="pack",
    )(*operands)


def solve(bounds, own, first, second):
    members, rows = own.shape[1], 4
    square = (rows, SPAN, SPAN)
    wide = pltpu.VMEM((rows, members, SPAN), jnp.float32)
    return pl.pallas_call(
        solve_kernel,
        out_shape=jax.ShapeDtypeStruct((own.shape[0] // CHUNK * 2 * rows, members), jnp.float32),
        in_specs=hbm(1) + vmem(3),
        out_specs=vmem(1)[0],
        scratch_shapes=[
            pltpu.VMEM((2, rows * SPAN, members), jnp.float32),
            pltpu.VMEM((LANES, members), jnp.float32),
            wide,
            pltpu.VMEM(square, jnp.float32),
            pltpu.VMEM(square, jnp.bfloat16),
            pltpu.VMEM(square, jnp.bfloat16),
            pltpu.VMEM((8, SPAN), jnp.float32),
            pltpu.VMEM((REACH + 1, 8, LANES), jnp.float32),
            pltpu.VMEM((REACH, 8, LANES), jnp.float32),
            pltpu.VMEM((META, SPAN), jnp.float32),
            wide,
            wide,
            wide,
            pltpu.SMEM(bounds.shape, jnp.float32),
            pltpu.SemaphoreType.DMA,
        ],
        compiler_params=PARAMS,
        name="solve",
    )(pltpu.with_memory_space_constraint(bounds, pltpu.HBM), own, first, second)


def on_device(ensemble, observed, obs_var, ridge, pred_back, bounds):
    local_blocks, rows, members = ensemble.shape
    slots = pred_back.shape[1]
    region_blocks = lax.axis_size("blk") * local_blocks
    regions = lax.axis_size("region")
    per_device = rows // lax.axis_size("blk")
    assert (local_blocks, per_device, members, region_blocks) == (2, 4, LANES, LANES)
    groups = rows // 8
    peers = 2 * groups
    packed = pack(pred_back, ridge, ensemble, observed, obs_var)
    own = lax.all_to_all(packed.reshape(peers, 1, CHUNK * members), "blk", 0, 0, tiled=True)
    edge = HALO // local_blocks

    odd = lax.axis_index("blk") % 2
    halo = []
    for turn in range(2):
        pairs = []
        for region in range(regions):
            for place in range(peers):
                target = region + (1 if place % 2 == turn else -1)
                if 0 <= target < regions:
                    pairs.append((region * peers + place, target * peers + place))
        start = jnp.where(odd == turn, peers - edge, 0)
        part = lax.dynamic_slice_in_dim(own, start, edge, 0)
        part = lax.ppermute(part, AXES, pairs)
        halo.append(part.reshape(edge * CHUNK, members))
    increment = solve(bounds, own.reshape(peers * CHUNK, members), *halo)
    increment = increment.reshape(2 * groups, local_blocks * per_device, members)
    increment = lax.all_to_all(increment, "blk", 0, 0, tiled=True)
    return pl.pallas_call(
        add_kernel,
        out_shape=jax.ShapeDtypeStruct(ensemble.shape, jnp.float32),
        in_specs=vmem(2),
        out_specs=vmem(1)[0],
        compiler_params=PARAMS,
        name="add",
    )(ensemble, increment.reshape(groups, 2, 8, members))


def solution(mesh):
    return jax.shard_map(
        on_device,
        mesh=mesh,
        in_specs=(
            P(AXES, None, None),
            P(AXES, None, None),
            P(AXES, None),
            P(AXES),
            P(AXES, None),
            P(),
        ),
        out_specs=P(AXES, None, None),
        check_vma=False,
    )
```

```python
import jax
import jax.numpy as jnp
from jax import lax
from jax.experimental import pallas as pl
from jax.experimental.pallas import tpu as pltpu
from jax.sharding import PartitionSpec as P

REACH = 16
ITERS = 3
HALO = ITERS * REACH
AXES = ("region", "blk")
LANES = 128
SPAN = 256
FIRST = 9
SECOND = 8
CHUNK = FIRST + SECOND
META = 16
HIGHEST = lax.Precision.HIGHEST
PARAMS = pltpu.CompilerParams(vmem_limit_bytes=48 * 1024 * 1024)


def iota(shape, axis):
    return lax.broadcasted_iota(jnp.int32, shape, axis)


def pack_kernel(
    pred_hbm, ridge_hbm, ens_hbm, obs_hbm, var_hbm, out_ref,
    pred_ref, ridge_ref, ens_ref, obs_ref, var_ref, sems,
):
    pairs = [
        (ens_hbm, ens_ref), (var_hbm, var_ref), (pred_hbm, pred_ref), (ridge_hbm, ridge_ref),
        (obs_hbm, obs_ref),
    ]
    copies = [pltpu.make_async_copy(a, b, sems.at[i]) for i, (a, b) in enumerate(pairs)]
    for copy in copies:
        copy.start()
    local_blocks, rows, members = ens_ref.shape
    slots = pred_ref.shape[1]
    last = members - 1
    groups = rows // 8
    low = iota((groups, 8, members), 1) < 4
    lane = iota((rows, members), 1)
    spot = iota((1, members), 1)

    def deal(blocks, start):
        blocks = [block.reshape(groups, 8, members) for block in blocks]
        even = jnp.where(low, blocks[0], pltpu.roll(blocks[1], 4, 1))
        odd = jnp.where(low, pltpu.roll(blocks[0], 4, 1), blocks[1])
        for q in range(groups):
            at = 2 * q * CHUNK + start
            out_ref[at : at + 8, :] = even[q]
            out_ref[at + CHUNK : at + CHUNK + 8, :] = odd[q]

    for copy in copies[:4]:
        copy.wait()
    meta = jnp.zeros((1, members), jnp.float32)
    blocks = []
    for b in range(local_blocks):
        for k in range(slots):
            meta = jnp.where(spot == META * b + k, pred_ref[b, k].astype(jnp.float32), meta)
        meta = jnp.where(spot == META * b + slots, ridge_ref[b], meta)
        ens = ens_ref[b]
        anomaly = (ens - jnp.mean(ens, axis=1, keepdims=True)) * (1.0 / (members - 1) ** 0.5)
        folded = anomaly + anomaly[:, last:] * (1.0 / (members**0.5 - 1.0))
        variance = jnp.broadcast_to(var_ref[b : b + 1, :], (members, rows)).T
        blocks.append(jnp.where(lane == last, variance, folded))
    deal(blocks, 0)
    for p in range(2 * groups):
        out_ref[p * CHUNK + FIRST - 1 : p * CHUNK + FIRST, :] = meta
    copies[4].wait()
    deal([obs_ref[b] - ens_ref[b] for b in range(local_blocks)], FIRST)


def add_kernel(ens_ref, inc_ref, out_ref):
    groups, _, _, members = inc_ref.shape
    low = iota((groups, 8, members), 1) < 4
    even, odd = inc_ref[:, 0], inc_ref[:, 1]
    shape = ens_ref.shape[1:]
    out_ref[0] = ens_ref[0] + jnp.where(low, even, pltpu.roll(odd, 4, 1)).reshape(shape)
    out_ref[1] = ens_ref[1] + jnp.where(low, pltpu.roll(even, 4, 1), odd).reshape(shape)


def solve_lags(gram, target):
    size = len(target)
    factor = {}
    inverse = []
    for j in range(size):
        for i in range(j, size):
            running = gram[i, j]
            for k in range(j):
                running = running - factor[i, k] * factor[j, k]
            if i == j:
                inverse.append(lax.rsqrt(running))
            else:
                factor[i, j] = running * inverse[j]
    forward = []
    for i in range(size):
        running = target[i]
        for k in range(i):
            running = running - factor[i, k] * forward[k]
        forward.append(running * inverse[i])
    beta = [None] * size
    for i in reversed(range(size)):
        running = forward[i]
        for k in range(i + 1, size):
            running = running - factor[k, i] * beta[k]
        beta[i] = running * inverse[i]
    return beta


def parity():
    return lax.axis_index("blk") % 2


def lag_sums(x, sums_ref, row):
    for lag in range(REACH + 1):
        other = pltpu.roll(x, lag, 1) if lag else x
        sums_ref[lag, row : row + 1, :] = jnp.sum(x * other, axis=0, keepdims=True)


def line_up(ref, tile_ref, at, parts=(0, 1), first=0, count=None):
    for s in range(first, first + (count or ref.shape[0] // CHUNK)):
        for part in parts:
            row = s * CHUNK + (0, FIRST)[part]
            tile_ref[part, 8 * at : 8 * (at + 1), :] = ref[row : row + 8, :]
        at += 1


def columns(tile_ref, r, x_ref, res_ref, inverse_ref, lanes):
    members = LANES
    x = tile_ref[0, pl.ds(r, LANES, stride=4), :].T
    variance = x[members - 1 :, :]
    inverse = 1.0 / jnp.where(variance > 0, variance, 1.0)
    x = jnp.where(iota((members, LANES), 0) == members - 1, 0.0, x)
    x_ref[r, :, lanes] = x
    res_ref[r, :, lanes] = tile_ref[1, pl.ds(r, LANES, stride=4), :].T * inverse
    inverse_ref[4 + r : 5 + r, lanes] = inverse
    return x


def local_kernel(own_ref, x_ref, res_ref, inverse_ref, sums_ref, tile_ref):
    line_up(own_ref, tile_ref, 0)
    inverse_ref[0:4, :] = jnp.zeros((4, LANES), jnp.float32)
    for r in range(4):
        x = columns(tile_ref, r, x_ref, res_ref, inverse_ref, slice(0, LANES))
        lag_sums(x, sums_ref, r)


def solve_kernel(
    bounds_hbm, own_ref, first_ref, second_ref, own_x_ref, own_res_ref, own_inverse_ref, own_sums_ref,
    out_ref,
    tile_ref, fact_ref, x_ref, exact_ref, high_ref, low_ref, inverse_ref,
    sums_ref, beta_ref, meta_ref, res_ref, dir_ref, inc_ref, bounds_ref, sem,
):
    copy = pltpu.make_async_copy(bounds_hbm, bounds_ref, sem)
    copy.start()
    edge = first_ref.shape[0] // CHUNK
    peers = own_ref.shape[0] // CHUNK
    reach = REACH // 2
    after, before, head = reach, reach + edge, reach + 2 * edge

    def facts(ref):
        return ref[pl.ds(FIRST - 1, ref.shape[0] // CHUNK, stride=CHUNK), :]

    own_facts = facts(own_ref)
    fact_ref[0:peers, :] = own_facts
    fact_ref[peers : peers + reach, :] = own_facts[peers - reach :]
    fact_ref[peers + head :, :] = own_facts[:reach]
    line_up(own_ref, tile_ref, 0, (0,), peers - reach, reach)
    line_up(own_ref, tile_ref, head, (0,), 0, reach)
    for at in (0, head):
        tile_ref[1, 8 * at : 8 * (at + reach), :] = jnp.zeros((8 * reach, LANES), jnp.float32)
    for turn in range(2):

        @pl.when(parity() == turn)
        def _():
            for ref, at in (((first_ref, second_ref)[turn], before), ((second_ref, first_ref)[turn], after)):
                line_up(ref, tile_ref, at)
                fact_ref[peers + at : peers + at + edge, :] = facts(ref)

    for r in range(4):
        x_ref[r, :, :LANES] = own_x_ref[r]
        res_ref[r, :, :LANES] = own_res_ref[r]
    inverse_ref[:, :LANES] = own_inverse_ref[...]
    for r in range(4):
        x = columns(tile_ref, r, x_ref, res_ref, inverse_ref, slice(LANES, SPAN))
        lag_sums(x, sums_ref, 4 + r)
    sums_ref[:, 0:4, :] = own_sums_ref[...]
    regress(fact_ref, high_ref, low_ref, inverse_ref, x_ref, exact_ref, sums_ref, beta_ref, meta_ref)
    copy.wait()
    iterate(bounds_ref, high_ref, low_ref, inverse_ref, out_ref, res_ref, dir_ref, inc_ref)


def regress(fact_ref, high_ref, low_ref, inverse_ref, x_ref, exact_ref, sums_ref, beta_ref, meta_ref):
    rows = 4
    slots = 12
    facts = fact_ref[...].T
    spread = iota((LANES, SPAN), 1) - 2 * iota((LANES, SPAN), 0)
    meta_ref[...] = sum(
        jnp.dot(
            facts[META * b : META * (b + 1), :],
            jnp.where(spread == b, 1.0, 0.0),
            precision=HIGHEST,
            preferred_element_type=jnp.float32,
        )
        for b in range(2)
    )

    upper_half = iota((8, LANES), 0) >= 4
    lane = iota((8, LANES), 1)

    def packed(k):
        return jnp.where(upper_half, meta_ref[k : k + 1, LANES:], meta_ref[k : k + 1, :LANES])

    def crossed(value):
        return pltpu.roll(pltpu.roll(value, REACH, 1), 4, 0)

    edge_lane = lane < REACH
    sums = [sums_ref[lag] for lag in range(REACH + 1)]
    sums = [jnp.where(edge_lane, crossed(value), value) for value in sums]

    picks = [packed(k) for k in range(slots)]
    ridge = packed(slots)
    used = []
    for lag in range(1, REACH + 1):
        hit = jnp.abs(picks[0] - lag) < 0.5
        for k in range(1, slots):
            hit = hit | (jnp.abs(picks[k] - lag) < 0.5)
        used.append(jnp.where(hit, 1.0, 0.0))
    gram = {}
    for i in range(REACH):
        for j in range(i):
            gram[i, j] = pltpu.roll(sums[i - j], j + 1, 1) * (used[i] * used[j])
        gram[i, i] = jnp.where(used[i] > 0, pltpu.roll(sums[0], i + 1, 1) + ridge, 1.0)
    target = [sums[i + 1] * used[i] for i in range(REACH)]
    beta = solve_lags(gram, target)
    known = (lane >= REACH) & (lane < REACH + HALO)
    known = known | ((lane >= HALO + 2 * REACH) & (lane < REACH + 2 * HALO))
    for i in range(REACH):
        value = jnp.where(edge_lane & ~upper_half, crossed(beta[i]), beta[i])
        beta_ref[i] = jnp.where(upper_half & ~known, 0.0, -value)

    def fill(row, count, half, lag_of):
        for at in range(row, row + count, 16):
            part = lag_of[at - row : at - row + 16]
            factors = [jnp.where(part == 0, 1.0, 0.0)] * rows
            for lag in range(1, REACH + 1):
                hit = part == lag
                for r in range(rows):
                    value = beta_ref[lag - 1, 4 * half + r : 4 * half + r + 1, :]
                    factors[r] = jnp.where(hit, value, factors[r])
            store(at, 16, half, factors)

    def store(row, count, half, factors):
        lanes = slice(half * LANES, (half + 1) * LANES)
        for r in range(rows):
            high = factors[r].astype(jnp.bfloat16)
            low = (factors[r] - high.astype(jnp.float32)).astype(jnp.bfloat16)
            exact_ref[r, row : row + count, lanes] = factors[r]
            high_ref[r, row : row + count, lanes] = high
            low_ref[r, row : row + count, lanes] = low

    square = (LANES, LANES)
    row, column = iota(square, 0), iota(square, 1)
    lag_of = column - row
    fill(0, LANES, 0, lag_of)
    copied = (row < REACH) | (row >= LANES - REACH)
    fill(LANES, LANES, 1, jnp.where(copied & (lag_of != 0), -1, lag_of))
    corner = column[:REACH] - row[:REACH]
    fill(LANES - REACH, REACH, 1, jnp.where(corner == 0, -1, corner))
    before_end = REACH + 2 * HALO
    corner = column[:REACH] - row[:REACH] + REACH
    fill(LANES + before_end - REACH, REACH, 0, corner)
    for start, stop, half in (
        (0, LANES - REACH, 1),
        (LANES, LANES + before_end - REACH, 0),
        (LANES + before_end, SPAN, 0),
    ):
        store(start, stop - start, half, [jnp.zeros((stop - start, LANES), jnp.float32)] * rows)

    for r in range(rows):
        resid = jnp.dot(
            x_ref[r], exact_ref[r], precision=HIGHEST, preferred_element_type=jnp.float32
        )
        total = jnp.sum(resid * resid, axis=0, keepdims=True)
        inverse_ref[r : r + 1, :] = 1.0 / (total + 1e-05)


def iterate(bounds_ref, high_ref, low_ref, inverse_ref, out_ref, res_ref, dir_ref, inc_ref):
    rows = 4
    members = LANES
    blocks = out_ref.shape[0] // rows
    lower = jnp.full((1, SPAN), bounds_ref[0], jnp.float32)
    higher = jnp.full((1, SPAN), bounds_ref[1], jnp.float32)
    theta = (higher + lower) / 2
    delta = (higher - lower) / 2
    sigma = theta / delta
    rho = 1.0 / sigma

    def product(value, r, axis):
        high = value.astype(jnp.bfloat16)
        low = (value - high.astype(jnp.float32)).astype(jnp.bfloat16)
        dims = (((1,), (axis,)), ((), ()))

        def dot(a, b):
            return lax.dot_general(a, b, dims, preferred_element_type=jnp.float32)

        both = dot(jnp.concatenate([high, low], axis=0), high_ref[r])
        return both[:members] + (both[members:] + dot(high, low_ref[r]))

    for r in range(rows):
        dir_ref[r] = res_ref[r] / theta
        inc_ref[r] = dir_ref[r]
    for _ in range(ITERS):
        rho_next = 1.0 / (2 * sigma - rho)
        for r in range(rows):
            direction = dir_ref[r]
            middle = product(direction, r, 0) * inverse_ref[r : r + 1, :]
            applied = product(middle, r, 1) + inverse_ref[4 + r : 5 + r, :] * direction
            residue = res_ref[r] - applied
            direction = (rho_next * rho) * direction + (2 * rho_next / delta) * residue
            res_ref[r] = residue
            dir_ref[r] = direction
            inc_ref[r] = inc_ref[r] + direction
        rho = rho_next
    for r in range(rows):
        out_ref[pl.ds(r, blocks, stride=rows), :] = inc_ref[r, :, :blocks].T


def vmem(count):
    return [pl.BlockSpec(memory_space=pltpu.VMEM)] * count


def hbm(count):
    return [pl.BlockSpec(memory_space=pltpu.HBM)] * count


def pack(pred_back, ridge, ensemble, observed, obs_var):
    local_blocks, rows, members = ensemble.shape
    peers = rows // 4
    operands = [
        pltpu.with_memory_space_constraint(value, pltpu.HBM)
        for value in (pred_back, ridge, ensemble, observed, obs_var)
    ]
    return pl.pallas_call(
        pack_kernel,
        out_shape=pltpu.VMEM((peers * CHUNK, members), jnp.float32),
        in_specs=hbm(5),
        out_specs=vmem(1)[0],
        scratch_shapes=[
            pltpu.SMEM(pred_back.shape, jnp.int32),
            pltpu.SMEM(ridge.shape, jnp.float32),
            pltpu.VMEM(ensemble.shape, jnp.float32),
            pltpu.VMEM(observed.shape, jnp.float32),
            pltpu.VMEM(obs_var.shape, jnp.float32),
            pltpu.SemaphoreType.DMA((5,)),
        ],
        compiler_params=PARAMS,
        name="pack",
    )(*operands)


def local(own):
    members = own.shape[1]
    flat = jax.ShapeDtypeStruct((4, members, LANES), jnp.float32)
    return pl.pallas_call(
        local_kernel,
        out_shape=[
            flat,
            flat,
            jax.ShapeDtypeStruct((8, LANES), jnp.float32),
            jax.ShapeDtypeStruct((REACH + 1, 4, LANES), jnp.float32),
        ],
        in_specs=vmem(1),
        out_specs=vmem(4),
        scratch_shapes=[pltpu.VMEM((2, 4 * LANES, members), jnp.float32)],
        compiler_params=PARAMS,
        name="local",
    )(own)


def solve(bounds, own, first, second, mine):
    members, rows = own.shape[1], 4
    square = (rows, SPAN, SPAN)
    wide = pltpu.VMEM((rows, members, SPAN), jnp.float32)
    return pl.pallas_call(
        solve_kernel,
        out_shape=jax.ShapeDtypeStruct((own.shape[0] // CHUNK * 2 * rows, members), jnp.float32),
        in_specs=hbm(1) + vmem(7),
        out_specs=vmem(1)[0],
        scratch_shapes=[
            pltpu.VMEM((2, rows * LANES, members), jnp.float32),
            pltpu.VMEM((LANES, members), jnp.float32),
            wide,
            pltpu.VMEM(square, jnp.float32),
            pltpu.VMEM(square, jnp.bfloat16),
            pltpu.VMEM(square, jnp.bfloat16),
            pltpu.VMEM((8, SPAN), jnp.float32),
            pltpu.VMEM((REACH + 1, 8, LANES), jnp.float32),
            pltpu.VMEM((REACH, 8, LANES), jnp.float32),
            pltpu.VMEM((META, SPAN), jnp.float32),
            wide,
            wide,
            wide,
            pltpu.SMEM(bounds.shape, jnp.float32),
            pltpu.SemaphoreType.DMA,
        ],
        compiler_params=PARAMS,
        name="solve",
    )(pltpu.with_memory_space_constraint(bounds, pltpu.HBM), own, first, second, *mine)


def on_device(ensemble, observed, obs_var, ridge, pred_back, bounds):
    local_blocks, rows, members = ensemble.shape
    slots = pred_back.shape[1]
    region_blocks = lax.axis_size("blk") * local_blocks
    regions = lax.axis_size("region")
    per_device = rows // lax.axis_size("blk")
    assert (local_blocks, per_device, members, region_blocks) == (2, 4, LANES, LANES)
    groups = rows // 8
    peers = 2 * groups
    packed = pack(pred_back, ridge, ensemble, observed, obs_var)
    own = lax.all_to_all(packed.reshape(peers, 1, CHUNK * members), "blk", 0, 0, tiled=True)
    edge = HALO // local_blocks

    odd = lax.axis_index("blk") % 2
    halo = []
    for turn in range(2):
        pairs = []
        for region in range(regions):
            for place in range(peers):
                target = region + (1 if place % 2 == turn else -1)
                if 0 <= target < regions:
                    pairs.append((region * peers + place, target * peers + place))
        start = jnp.where(odd == turn, peers - edge, 0)
        part = lax.dynamic_slice_in_dim(own, start, edge, 0)
        part = lax.ppermute(part, AXES, pairs)
        halo.append(part.reshape(edge * CHUNK, members))
    own = own.reshape(peers * CHUNK, members)
    increment = solve(bounds, own, *halo, local(own))
    increment = increment.reshape(2 * groups, local_blocks * per_device, members)
    increment = lax.all_to_all(increment, "blk", 0, 0, tiled=True)
    return pl.pallas_call(
        add_kernel,
        out_shape=jax.ShapeDtypeStruct(ensemble.shape, jnp.float32),
        in_specs=vmem(2),
        out_specs=vmem(1)[0],
        compiler_params=PARAMS,
        name="add",
    )(ensemble, increment.reshape(groups, 2, 8, members))


def solution(mesh):
    return jax.shard_map(
        on_device,
        mesh=mesh,
        in_specs=(
            P(AXES, None, None),
            P(AXES, None, None),
            P(AXES, None),
            P(AXES),
            P(AXES, None),
            P(),
        ),
        out_specs=P(AXES, None, None),
        check_vma=False,
    )
```

```python
import jax
import jax.numpy as jnp
from jax import lax
from jax.experimental import pallas as pl
from jax.experimental.pallas import tpu as pltpu
from jax.sharding import PartitionSpec as P

REACH = 16
ITERS = 3
HALO = ITERS * REACH
AXES = ("region", "blk")
LANES = 128
SPAN = 256
FIRST = 9
SECOND = 8
CHUNK = FIRST + SECOND
META = 16
HIGHEST = lax.Precision.HIGHEST
PARAMS = pltpu.CompilerParams(vmem_limit_bytes=48 * 1024 * 1024)


def iota(shape, axis):
    return lax.broadcasted_iota(jnp.int32, shape, axis)


def pack_kernel(
    pred_hbm, ridge_hbm, ens_hbm, obs_hbm, var_hbm, out_ref,
    pred_ref, ridge_ref, ens_ref, obs_ref, var_ref, sems,
):
    pairs = [
        (ens_hbm, ens_ref), (var_hbm, var_ref), (pred_hbm, pred_ref), (ridge_hbm, ridge_ref),
        (obs_hbm, obs_ref),
    ]
    copies = [pltpu.make_async_copy(a, b, sems.at[i]) for i, (a, b) in enumerate(pairs)]
    for copy in copies:
        copy.start()
    local_blocks, rows, members = ens_ref.shape
    slots = pred_ref.shape[1]
    last = members - 1
    groups = rows // 8
    low = iota((groups, 8, members), 1) < 4
    lane = iota((rows, members), 1)
    spot = iota((1, members), 1)

    def deal(blocks, start):
        blocks = [block.reshape(groups, 8, members) for block in blocks]
        even = jnp.where(low, blocks[0], pltpu.roll(blocks[1], 4, 1))
        odd = jnp.where(low, pltpu.roll(blocks[0], 4, 1), blocks[1])
        for q in range(groups):
            at = 2 * q * CHUNK + start
            out_ref[at : at + 8, :] = even[q]
            out_ref[at + CHUNK : at + CHUNK + 8, :] = odd[q]

    for copy in copies[:4]:
        copy.wait()
    meta = jnp.zeros((1, members), jnp.float32)
    blocks = []
    for b in range(local_blocks):
        for k in range(slots):
            meta = jnp.where(spot == META * b + k, pred_ref[b, k].astype(jnp.float32), meta)
        meta = jnp.where(spot == META * b + slots, ridge_ref[b], meta)
        ens = ens_ref[b]
        anomaly = (ens - jnp.mean(ens, axis=1, keepdims=True)) * (1.0 / (members - 1) ** 0.5)
        folded = anomaly + anomaly[:, last:] * (1.0 / (members**0.5 - 1.0))
        variance = jnp.broadcast_to(var_ref[b : b + 1, :], (members, rows)).T
        blocks.append(jnp.where(lane == last, variance, folded))
    deal(blocks, 0)
    for p in range(2 * groups):
        out_ref[p * CHUNK + FIRST - 1 : p * CHUNK + FIRST, :] = meta
    copies[4].wait()
    deal([obs_ref[b] - ens_ref[b] for b in range(local_blocks)], FIRST)


def add_kernel(ens_ref, inc_ref, out_ref):
    groups, _, _, members = inc_ref.shape
    low = iota((groups, 8, members), 1) < 4
    even, odd = inc_ref[:, 0], inc_ref[:, 1]
    shape = ens_ref.shape[1:]
    out_ref[0] = ens_ref[0] + jnp.where(low, even, pltpu.roll(odd, 4, 1)).reshape(shape)
    out_ref[1] = ens_ref[1] + jnp.where(low, pltpu.roll(even, 4, 1), odd).reshape(shape)


def solve_lags(gram, target):
    size = len(target)
    factor = {}
    inverse = []
    for j in range(size):
        for i in range(j, size):
            running = gram[i, j]
            for k in range(j):
                running = running - factor[i, k] * factor[j, k]
            if i == j:
                inverse.append(lax.rsqrt(running))
            else:
                factor[i, j] = running * inverse[j]
    forward = []
    for i in range(size):
        running = target[i]
        for k in range(i):
            running = running - factor[i, k] * forward[k]
        forward.append(running * inverse[i])
    beta = [None] * size
    for i in reversed(range(size)):
        running = forward[i]
        for k in range(i + 1, size):
            running = running - factor[k, i] * beta[k]
        beta[i] = running * inverse[i]
    return beta


def parity():
    return lax.axis_index("blk") % 2


def lag_sums(x, sums_ref, row):
    for lag in range(REACH + 1):
        other = pltpu.roll(x, lag, 1) if lag else x
        sums_ref[lag, row : row + 1, :] = jnp.sum(x * other, axis=0, keepdims=True)


def line_up(ref, tile_ref, at, parts=(0, 1), first=0, count=None):
    for s in range(first, first + (count or ref.shape[0] // CHUNK)):
        for part in parts:
            row = s * CHUNK + (0, FIRST)[part]
            tile_ref[part, 8 * at : 8 * (at + 1), :] = ref[row : row + 8, :]
        at += 1


def columns(tile_ref, r, x_ref, res_ref, inverse_ref, lanes):
    members = LANES
    x = tile_ref[0, pl.ds(r, LANES, stride=4), :].T
    variance = x[members - 1 :, :]
    inverse = 1.0 / jnp.where(variance > 0, variance, 1.0)
    x = jnp.where(iota((members, LANES), 0) == members - 1, 0.0, x)
    x_ref[r, :, lanes] = x
    res_ref[r, :, lanes] = tile_ref[1, pl.ds(r, LANES, stride=4), :].T * inverse
    inverse_ref[4 + r : 5 + r, lanes] = inverse
    return x


def local_kernel(own_ref, x_ref, res_ref, inverse_ref, sums_ref, tile_ref):
    line_up(own_ref, tile_ref, 0)
    inverse_ref[0:4, :] = jnp.zeros((4, LANES), jnp.float32)
    for r in range(4):
        x = columns(tile_ref, r, x_ref, res_ref, inverse_ref, slice(0, LANES))
        lag_sums(x, sums_ref, r)


def solve_kernel(
    bounds_hbm, own_ref, first_ref, second_ref, own_x_ref, own_res_ref, own_inverse_ref, own_sums_ref,
    out_ref,
    tile_ref, fact_ref, x_ref, exact_ref, high_ref, low_ref, inverse_ref,
    sums_ref, beta_ref, meta_ref, res_ref, dir_ref, inc_ref, bounds_ref, sem,
):
    copy = pltpu.make_async_copy(bounds_hbm, bounds_ref, sem)
    copy.start()
    edge = first_ref.shape[0] // CHUNK
    peers = own_ref.shape[0] // CHUNK
    reach = REACH // 2
    after, before, head = reach, reach + edge, reach + 2 * edge

    def facts(ref):
        return ref[pl.ds(FIRST - 1, ref.shape[0] // CHUNK, stride=CHUNK), :]

    own_facts = facts(own_ref)
    fact_ref[0:peers, :] = own_facts
    fact_ref[peers : peers + reach, :] = own_facts[peers - reach :]
    fact_ref[peers + head :, :] = own_facts[:reach]
    line_up(own_ref, tile_ref, 0, (0,), peers - reach, reach)
    line_up(own_ref, tile_ref, head, (0,), 0, reach)
    for at in (0, head):
        tile_ref[1, 8 * at : 8 * (at + reach), :] = jnp.zeros((8 * reach, LANES), jnp.float32)
    for turn in range(2):

        @pl.when(parity() == turn)
        def _():
            for ref, at in (((first_ref, second_ref)[turn], before), ((second_ref, first_ref)[turn], after)):
                line_up(ref, tile_ref, at)
                fact_ref[peers + at : peers + at + edge, :] = facts(ref)

    for r in range(4):
        x_ref[r, :, :LANES] = own_x_ref[r]
        res_ref[r, :, :LANES] = own_res_ref[r]
    inverse_ref[:, :LANES] = own_inverse_ref[...]
    for r in range(4):
        x = columns(tile_ref, r, x_ref, res_ref, inverse_ref, slice(LANES, SPAN))
        lag_sums(x, sums_ref, 4 + r)
    sums_ref[:, 0:4, :] = own_sums_ref[...]
    regress(fact_ref, high_ref, low_ref, inverse_ref, x_ref, exact_ref, sums_ref, beta_ref, meta_ref)
    copy.wait()
    iterate(bounds_ref, high_ref, low_ref, inverse_ref, out_ref, res_ref, dir_ref, inc_ref)


def regress(fact_ref, high_ref, low_ref, inverse_ref, x_ref, exact_ref, sums_ref, beta_ref, meta_ref):
    rows = 4
    slots = 12
    facts = fact_ref[...].T
    spread = iota((LANES, SPAN), 1) - 2 * iota((LANES, SPAN), 0)
    meta_ref[...] = sum(
        jnp.dot(
            facts[META * b : META * (b + 1), :],
            jnp.where(spread == b, 1.0, 0.0),
            precision=HIGHEST,
            preferred_element_type=jnp.float32,
        )
        for b in range(2)
    )

    upper_half = iota((8, LANES), 0) >= 4
    lane = iota((8, LANES), 1)

    def packed(k):
        return jnp.where(upper_half, meta_ref[k : k + 1, LANES:], meta_ref[k : k + 1, :LANES])

    def crossed(value):
        return pltpu.roll(pltpu.roll(value, REACH, 1), 4, 0)

    edge_lane = lane < REACH
    sums = [sums_ref[lag] for lag in range(REACH + 1)]
    sums = [jnp.where(edge_lane, crossed(value), value) for value in sums]

    picks = [packed(k) for k in range(slots)]
    ridge = packed(slots)
    used = []
    for lag in range(1, REACH + 1):
        hit = jnp.abs(picks[0] - lag) < 0.5
        for k in range(1, slots):
            hit = hit | (jnp.abs(picks[k] - lag) < 0.5)
        used.append(jnp.where(hit, 1.0, 0.0))
    gram = {}
    for i in range(REACH):
        for j in range(i):
            gram[i, j] = pltpu.roll(sums[i - j], j + 1, 1) * (used[i] * used[j])
        gram[i, i] = jnp.where(used[i] > 0, pltpu.roll(sums[0], i + 1, 1) + ridge, 1.0)
    target = [sums[i + 1] * used[i] for i in range(REACH)]
    beta = solve_lags(gram, target)
    known = (lane >= REACH) & (lane < REACH + HALO)
    known = known | ((lane >= HALO + 2 * REACH) & (lane < REACH + 2 * HALO))
    for i in range(REACH):
        value = jnp.where(edge_lane & ~upper_half, crossed(beta[i]), beta[i])
        beta_ref[i] = jnp.where(upper_half & ~known, 0.0, -value)

    def fill(row, count, half, lag_of):
        for at in range(row, row + count, 16):
            part = lag_of[at - row : at - row + 16]
            factors = [jnp.where(part == 0, 1.0, 0.0)] * rows
            for lag in range(1, REACH + 1):
                hit = part == lag
                for r in range(rows):
                    value = beta_ref[lag - 1, 4 * half + r : 4 * half + r + 1, :]
                    factors[r] = jnp.where(hit, value, factors[r])
            store(at, 16, half, factors)

    def store(row, count, half, factors):
        lanes = slice(half * LANES, (half + 1) * LANES)
        for r in range(rows):
            high = factors[r].astype(jnp.bfloat16)
            low = (factors[r] - high.astype(jnp.float32)).astype(jnp.bfloat16)
            exact_ref[r, row : row + count, lanes] = factors[r]
            high_ref[r, row : row + count, lanes] = high
            low_ref[r, row : row + count, lanes] = low

    square = (LANES, LANES)
    row, column = iota(square, 0), iota(square, 1)
    lag_of = column - row
    fill(0, LANES, 0, lag_of)
    copied = (row < REACH) | (row >= LANES - REACH)
    fill(LANES, LANES, 1, jnp.where(copied & (lag_of != 0), -1, lag_of))
    corner = column[:REACH] - row[:REACH]
    fill(LANES - REACH, REACH, 1, jnp.where(corner == 0, -1, corner))
    before_end = REACH + 2 * HALO
    corner = column[:REACH] - row[:REACH] + REACH
    fill(LANES + before_end - REACH, REACH, 0, corner)
    for start, stop, half in (
        (0, LANES - REACH, 1),
        (LANES, LANES + before_end - REACH, 0),
        (LANES + before_end, SPAN, 0),
    ):
        store(start, stop - start, half, [jnp.zeros((stop - start, LANES), jnp.float32)] * rows)

    for r in range(rows):
        resid = jnp.dot(
            x_ref[r], exact_ref[r], precision=HIGHEST, preferred_element_type=jnp.float32
        )
        total = jnp.sum(resid * resid, axis=0, keepdims=True)
        inverse_ref[r : r + 1, :] = 1.0 / (total + 1e-05)


def iterate(bounds_ref, high_ref, low_ref, inverse_ref, out_ref, res_ref, dir_ref, inc_ref):
    rows = 4
    members = LANES
    blocks = out_ref.shape[0] // rows
    lower = jnp.full((1, SPAN), bounds_ref[0], jnp.float32)
    higher = jnp.full((1, SPAN), bounds_ref[1], jnp.float32)
    theta = (higher + lower) / 2
    delta = (higher - lower) / 2
    sigma = theta / delta
    rho = 1.0 / sigma

    def product(value, r, axis):
        high = value.astype(jnp.bfloat16)
        low = (value - high.astype(jnp.float32)).astype(jnp.bfloat16)
        dims = (((1,), (axis,)), ((), ()))

        def dot(a, b):
            return lax.dot_general(a, b, dims, preferred_element_type=jnp.float32)

        both = dot(jnp.concatenate([high, low], axis=0), high_ref[r])
        return both[:members] + (both[members:] + dot(high, low_ref[r]))

    for r in range(rows):
        dir_ref[r] = res_ref[r] / theta
        inc_ref[r] = dir_ref[r]
    for _ in range(ITERS):
        rho_next = 1.0 / (2 * sigma - rho)
        for r in range(rows):
            direction = dir_ref[r]
            middle = product(direction, r, 0) * inverse_ref[r : r + 1, :]
            applied = product(middle, r, 1) + inverse_ref[4 + r : 5 + r, :] * direction
            residue = res_ref[r] - applied
            direction = (rho_next * rho) * direction + (2 * rho_next / delta) * residue
            res_ref[r] = residue
            dir_ref[r] = direction
            inc_ref[r] = inc_ref[r] + direction
        rho = rho_next
    for r in range(rows):
        out_ref[pl.ds(r, blocks, stride=rows), :] = inc_ref[r, :, :blocks].T


def vmem(count):
    return [pl.BlockSpec(memory_space=pltpu.VMEM)] * count


def hbm(count):
    return [pl.BlockSpec(memory_space=pltpu.HBM)] * count


def pack(pred_back, ridge, ensemble, observed, obs_var):
    local_blocks, rows, members = ensemble.shape
    peers = rows // 4
    operands = [
        pltpu.with_memory_space_constraint(value, pltpu.HBM)
        for value in (pred_back, ridge, ensemble, observed, obs_var)
    ]
    return pl.pallas_call(
        pack_kernel,
        out_shape=pltpu.VMEM((peers * CHUNK, members), jnp.float32),
        in_specs=hbm(5),
        out_specs=vmem(1)[0],
        scratch_shapes=[
            pltpu.SMEM(pred_back.shape, jnp.int32),
            pltpu.SMEM(ridge.shape, jnp.float32),
            pltpu.VMEM(ensemble.shape, jnp.float32),
            pltpu.VMEM(observed.shape, jnp.float32),
            pltpu.VMEM(obs_var.shape, jnp.float32),
            pltpu.SemaphoreType.DMA((5,)),
        ],
        compiler_params=PARAMS,
        name="pack",
    )(*operands)


def local(own):
    members = own.shape[1]
    flat = jax.ShapeDtypeStruct((4, members, LANES), jnp.float32)
    return pl.pallas_call(
        local_kernel,
        out_shape=[
            flat,
            flat,
            jax.ShapeDtypeStruct((8, LANES), jnp.float32),
            jax.ShapeDtypeStruct((REACH + 1, 4, LANES), jnp.float32),
        ],
        in_specs=vmem(1),
        out_specs=vmem(4),
        scratch_shapes=[pltpu.VMEM((2, 4 * LANES, members), jnp.float32)],
        compiler_params=PARAMS,
        name="local",
    )(own)


def solve(bounds, own, first, second, mine):
    members, rows = own.shape[1], 4
    square = (rows, SPAN, SPAN)
    wide = pltpu.VMEM((rows, members, SPAN), jnp.float32)
    return pl.pallas_call(
        solve_kernel,
        out_shape=jax.ShapeDtypeStruct((own.shape[0] // CHUNK * 2 * rows, members), jnp.float32),
        in_specs=hbm(1) + vmem(7),
        out_specs=vmem(1)[0],
        scratch_shapes=[
            pltpu.VMEM((2, rows * LANES, members), jnp.float32),
            pltpu.VMEM((LANES, members), jnp.float32),
            wide,
            pltpu.VMEM(square, jnp.float32),
            pltpu.VMEM(square, jnp.bfloat16),
            pltpu.VMEM(square, jnp.bfloat16),
            pltpu.VMEM((8, SPAN), jnp.float32),
            pltpu.VMEM((REACH + 1, 8, LANES), jnp.float32),
            pltpu.VMEM((REACH, 8, LANES), jnp.float32),
            pltpu.VMEM((META, SPAN), jnp.float32),
            wide,
            wide,
            wide,
            pltpu.SMEM(bounds.shape, jnp.float32),
            pltpu.SemaphoreType.DMA,
        ],
        compiler_params=PARAMS,
        name="solve",
    )(pltpu.with_memory_space_constraint(bounds, pltpu.HBM), own, first, second, *mine)


def on_device(ensemble, observed, obs_var, ridge, pred_back, bounds):
    local_blocks, rows, members = ensemble.shape
    slots = pred_back.shape[1]
    region_blocks = lax.axis_size("blk") * local_blocks
    regions = lax.axis_size("region")
    per_device = rows // lax.axis_size("blk")
    assert (local_blocks, per_device, members, region_blocks) == (2, 4, LANES, LANES)
    groups = rows // 8
    peers = 2 * groups
    odd = (lax.axis_index("blk") & 1).astype(jnp.uint32)
    edge = HALO // local_blocks
    starts = [(1 - odd) * (peers - edge), odd * (peers - edge)]
    observed, *starts = lax.optimization_barrier((observed, *starts))
    packed = pack(pred_back, ridge, ensemble, observed, obs_var)
    own = lax.all_to_all(packed.reshape(peers, 1, CHUNK * members), "blk", 0, 0, tiled=True)
    flat = own.reshape(peers * CHUNK, members)
    mine = local(flat)
    halo = []
    for turn in range(2):
        pairs = []
        for region in range(regions):
            for place in range(peers):
                target = region + (1 if place % 2 == turn else -1)
                if 0 <= target < regions:
                    pairs.append((region * peers + place, target * peers + place))
        none = jnp.uint32(0)
        part = lax.dynamic_slice(own, (starts[turn], none, none), (edge, 1, own.shape[2]))
        if turn == 1:
            part, *mine = lax.optimization_barrier((part, *mine))
        part = lax.ppermute(part, AXES, pairs)
        halo.append(part.reshape(edge * CHUNK, members))
    increment = solve(bounds, flat, *halo, mine)
    increment = increment.reshape(2 * groups, local_blocks * per_device, members)
    increment = lax.all_to_all(increment, "blk", 0, 0, tiled=True)
    return pl.pallas_call(
        add_kernel,
        out_shape=jax.ShapeDtypeStruct(ensemble.shape, jnp.float32),
        in_specs=vmem(2),
        out_specs=vmem(1)[0],
        compiler_params=PARAMS,
        name="add",
    )(ensemble, increment.reshape(groups, 2, 8, members))


def solution(mesh):
    return jax.shard_map(
        on_device,
        mesh=mesh,
        in_specs=(
            P(AXES, None, None),
            P(AXES, None, None),
            P(AXES, None),
            P(AXES),
            P(AXES, None),
            P(),
        ),
        out_specs=P(AXES, None, None),
        check_vma=False,
    )
```

```python
import jax
import jax.numpy as jnp
from jax import lax
from jax.experimental import pallas as pl
from jax.experimental.pallas import tpu as pltpu
from jax.sharding import PartitionSpec as P

REACH = 16
ITERS = 3
HALO = ITERS * REACH
AXES = ("region", "blk")
LANES = 128
SPAN = 256
FIRST = 9
SECOND = 8
CHUNK = FIRST + SECOND
META = 16
HIGHEST = lax.Precision.HIGHEST
PARAMS = pltpu.CompilerParams(vmem_limit_bytes=48 * 1024 * 1024)


def iota(shape, axis):
    return lax.broadcasted_iota(jnp.int32, shape, axis)


def pack_kernel(
    pred_hbm, ridge_hbm, ens_hbm, obs_hbm, var_hbm, out_ref,
    pred_ref, ridge_ref, ens_ref, obs_ref, var_ref, sems,
):
    pairs = [
        (ens_hbm, ens_ref), (var_hbm, var_ref), (pred_hbm, pred_ref), (ridge_hbm, ridge_ref),
        (obs_hbm, obs_ref),
    ]
    copies = [pltpu.make_async_copy(a, b, sems.at[i]) for i, (a, b) in enumerate(pairs)]
    for copy in copies:
        copy.start()
    local_blocks, rows, members = ens_ref.shape
    slots = pred_ref.shape[1]
    last = members - 1
    groups = rows // 8
    low = iota((groups, 8, members), 1) < 4
    lane = iota((rows, members), 1)
    spot = iota((1, members), 1)

    def deal(blocks, start):
        blocks = [block.reshape(groups, 8, members) for block in blocks]
        even = jnp.where(low, blocks[0], pltpu.roll(blocks[1], 4, 1))
        odd = jnp.where(low, pltpu.roll(blocks[0], 4, 1), blocks[1])
        for q in range(groups):
            at = 2 * q * CHUNK + start
            out_ref[at : at + 8, :] = even[q]
            out_ref[at + CHUNK : at + CHUNK + 8, :] = odd[q]

    for copy in copies[:4]:
        copy.wait()
    meta = jnp.zeros((1, members), jnp.float32)
    blocks = []
    for b in range(local_blocks):
        for k in range(slots):
            meta = jnp.where(spot == META * b + k, pred_ref[b, k].astype(jnp.float32), meta)
        meta = jnp.where(spot == META * b + slots, ridge_ref[b], meta)
        ens = ens_ref[b]
        anomaly = (ens - jnp.mean(ens, axis=1, keepdims=True)) * (1.0 / (members - 1) ** 0.5)
        folded = anomaly + anomaly[:, last:] * (1.0 / (members**0.5 - 1.0))
        variance = jnp.broadcast_to(var_ref[b : b + 1, :], (members, rows)).T
        blocks.append(jnp.where(lane == last, variance, folded))
    deal(blocks, 0)
    for p in range(2 * groups):
        out_ref[p * CHUNK + FIRST - 1 : p * CHUNK + FIRST, :] = meta
    copies[4].wait()
    deal([obs_ref[b] - ens_ref[b] for b in range(local_blocks)], FIRST)


def add_kernel(ens_ref, inc_ref, out_ref):
    groups, _, _, members = inc_ref.shape
    low = iota((groups, 8, members), 1) < 4
    even, odd = inc_ref[:, 0], inc_ref[:, 1]
    shape = ens_ref.shape[1:]
    out_ref[0] = ens_ref[0] + jnp.where(low, even, pltpu.roll(odd, 4, 1)).reshape(shape)
    out_ref[1] = ens_ref[1] + jnp.where(low, pltpu.roll(even, 4, 1), odd).reshape(shape)


def solve_lags(gram, target):
    size = len(target)
    factor = {}
    inverse = []
    for j in range(size):
        for i in range(j, size):
            running = gram[i, j]
            for k in range(j):
                running = running - factor[i, k] * factor[j, k]
            if i == j:
                inverse.append(lax.rsqrt(running))
            else:
                factor[i, j] = running * inverse[j]
    forward = []
    for i in range(size):
        running = target[i]
        for k in range(i):
            running = running - factor[i, k] * forward[k]
        forward.append(running * inverse[i])
    beta = [None] * size
    for i in reversed(range(size)):
        running = forward[i]
        for k in range(i + 1, size):
            running = running - factor[k, i] * beta[k]
        beta[i] = running * inverse[i]
    return beta


def parity():
    return lax.axis_index("blk") % 2


def lag_sums(x, sums_ref, row):
    for lag in range(REACH + 1):
        other = pltpu.roll(x, lag, 1) if lag else x
        sums_ref[lag, row : row + 1, :] = jnp.sum(x * other, axis=0, keepdims=True)


def line_up(ref, tile_ref, at, parts=(0, 1), first=0, count=None):
    for s in range(first, first + (count or ref.shape[0] // CHUNK)):
        for part in parts:
            row = s * CHUNK + (0, FIRST)[part]
            tile_ref[part, 8 * at : 8 * (at + 1), :] = ref[row : row + 8, :]
        at += 1


def columns(tile_ref, r, x_ref, res_ref, inverse_ref, lanes):
    members = LANES
    x = tile_ref[0, pl.ds(r, LANES, stride=4), :].T
    variance = x[members - 1 :, :]
    inverse = 1.0 / jnp.where(variance > 0, variance, 1.0)
    x = jnp.where(iota((members, LANES), 0) == members - 1, 0.0, x)
    x_ref[r, :, lanes] = x
    res_ref[r, :, lanes] = tile_ref[1, pl.ds(r, LANES, stride=4), :].T * inverse
    inverse_ref[4 + r : 5 + r, lanes] = inverse
    return x


def local_kernel(own_ref, x_ref, res_ref, inverse_ref, sums_ref, tile_ref):
    line_up(own_ref, tile_ref, 0)
    inverse_ref[0:4, :] = jnp.zeros((4, LANES), jnp.float32)
    for r in range(4):
        x = columns(tile_ref, r, x_ref, res_ref, inverse_ref, slice(0, LANES))
        lag_sums(x, sums_ref, r)


def solve_kernel(
    bounds_hbm, own_ref, first_ref, second_ref, own_x_ref, own_res_ref, own_inverse_ref, own_sums_ref,
    out_ref,
    tile_ref, fact_ref, x_ref, exact_ref, high_ref, low_ref, inverse_ref,
    sums_ref, beta_ref, meta_ref, res_ref, dir_ref, inc_ref, bounds_ref, sem,
):
    copy = pltpu.make_async_copy(bounds_hbm, bounds_ref, sem)
    copy.start()
    edge = first_ref.shape[0] // CHUNK
    peers = own_ref.shape[0] // CHUNK
    reach = REACH // 2
    after, before, head = reach, reach + edge, reach + 2 * edge

    def facts(ref):
        return ref[pl.ds(FIRST - 1, ref.shape[0] // CHUNK, stride=CHUNK), :]

    own_facts = facts(own_ref)
    fact_ref[0:peers, :] = own_facts
    fact_ref[peers : peers + reach, :] = own_facts[peers - reach :]
    fact_ref[peers + head :, :] = own_facts[:reach]
    line_up(own_ref, tile_ref, 0, (0,), peers - reach, reach)
    line_up(own_ref, tile_ref, head, (0,), 0, reach)
    for at in (0, head):
        tile_ref[1, 8 * at : 8 * (at + reach), :] = jnp.zeros((8 * reach, LANES), jnp.float32)
    for turn in range(2):

        @pl.when(parity() == turn)
        def _():
            for ref, at in (((first_ref, second_ref)[turn], before), ((second_ref, first_ref)[turn], after)):
                line_up(ref, tile_ref, at)
                fact_ref[peers + at : peers + at + edge, :] = facts(ref)

    for r in range(4):
        x_ref[r, :, :LANES] = own_x_ref[r]
        res_ref[r, :, :LANES] = own_res_ref[r]
    inverse_ref[:, :LANES] = own_inverse_ref[...]
    for r in range(4):
        x = columns(tile_ref, r, x_ref, res_ref, inverse_ref, slice(LANES, SPAN))
        lag_sums(x, sums_ref, 4 + r)
    sums_ref[:, 0:4, :] = own_sums_ref[...]
    regress(fact_ref, high_ref, low_ref, inverse_ref, x_ref, exact_ref, sums_ref, beta_ref, meta_ref)
    copy.wait()
    iterate(bounds_ref, high_ref, low_ref, inverse_ref, out_ref, res_ref, dir_ref, inc_ref)


def regress(fact_ref, high_ref, low_ref, inverse_ref, x_ref, exact_ref, sums_ref, beta_ref, meta_ref):
    rows = 4
    slots = 12
    facts = fact_ref[...].T
    spread = iota((LANES, SPAN), 1) - 2 * iota((LANES, SPAN), 0)
    meta_ref[...] = sum(
        jnp.dot(
            facts[META * b : META * (b + 1), :],
            jnp.where(spread == b, 1.0, 0.0),
            precision=HIGHEST,
            preferred_element_type=jnp.float32,
        )
        for b in range(2)
    )

    upper_half = iota((8, LANES), 0) >= 4
    lane = iota((8, LANES), 1)

    def packed(k):
        return jnp.where(upper_half, meta_ref[k : k + 1, LANES:], meta_ref[k : k + 1, :LANES])

    def crossed(value):
        return pltpu.roll(pltpu.roll(value, REACH, 1), 4, 0)

    edge_lane = lane < REACH
    sums = [sums_ref[lag] for lag in range(REACH + 1)]
    sums = [jnp.where(edge_lane, crossed(value), value) for value in sums]

    picks = [packed(k) for k in range(slots)]
    ridge = packed(slots)
    used = []
    for lag in range(1, REACH + 1):
        hit = jnp.abs(picks[0] - lag) < 0.5
        for k in range(1, slots):
            hit = hit | (jnp.abs(picks[k] - lag) < 0.5)
        used.append(jnp.where(hit, 1.0, 0.0))
    gram = {}
    for i in range(REACH):
        for j in range(i):
            gram[i, j] = pltpu.roll(sums[i - j], j + 1, 1) * (used[i] * used[j])
        gram[i, i] = jnp.where(used[i] > 0, pltpu.roll(sums[0], i + 1, 1) + ridge, 1.0)
    target = [sums[i + 1] * used[i] for i in range(REACH)]
    beta = solve_lags(gram, target)
    known = (lane >= REACH) & (lane < REACH + HALO)
    known = known | ((lane >= HALO + 2 * REACH) & (lane < REACH + 2 * HALO))
    for i in range(REACH):
        value = jnp.where(edge_lane & ~upper_half, crossed(beta[i]), beta[i])
        beta_ref[i] = jnp.where(upper_half & ~known, 0.0, -value)

    def fill(row, count, half, lag_of):
        for at in range(row, row + count, 16):
            part = lag_of[at - row : at - row + 16]
            factors = [jnp.where(part == 0, 1.0, 0.0)] * rows
            for lag in range(1, REACH + 1):
                hit = part == lag
                for r in range(rows):
                    value = beta_ref[lag - 1, 4 * half + r : 4 * half + r + 1, :]
                    factors[r] = jnp.where(hit, value, factors[r])
            store(at, 16, half, factors)

    def store(row, count, half, factors):
        lanes = slice(half * LANES, (half + 1) * LANES)
        for r in range(rows):
            high = factors[r].astype(jnp.bfloat16)
            low = (factors[r] - high.astype(jnp.float32)).astype(jnp.bfloat16)
            exact_ref[r, row : row + count, lanes] = factors[r]
            high_ref[r, row : row + count, lanes] = high
            low_ref[r, row : row + count, lanes] = low

    square = (LANES, LANES)
    row, column = iota(square, 0), iota(square, 1)
    lag_of = column - row
    fill(0, LANES, 0, lag_of)
    copied = (row < REACH) | (row >= LANES - REACH)
    fill(LANES, LANES, 1, jnp.where(copied & (lag_of != 0), -1, lag_of))
    corner = column[:REACH] - row[:REACH]
    fill(LANES - REACH, REACH, 1, jnp.where(corner == 0, -1, corner))
    before_end = REACH + 2 * HALO
    corner = column[:REACH] - row[:REACH] + REACH
    fill(LANES + before_end - REACH, REACH, 0, corner)
    for start, stop, half in (
        (0, LANES - REACH, 1),
        (LANES, LANES + before_end - REACH, 0),
        (LANES + before_end, SPAN, 0),
    ):
        store(start, stop - start, half, [jnp.zeros((stop - start, LANES), jnp.float32)] * rows)

    for r in range(rows):
        resid = jnp.dot(
            x_ref[r], exact_ref[r], precision=HIGHEST, preferred_element_type=jnp.float32
        )
        total = jnp.sum(resid * resid, axis=0, keepdims=True)
        inverse_ref[r : r + 1, :] = 1.0 / (total + 1e-05)


def iterate(bounds_ref, high_ref, low_ref, inverse_ref, out_ref, res_ref, dir_ref, inc_ref):
    rows = 4
    members = LANES
    blocks = out_ref.shape[0] // rows
    lower = jnp.full((1, SPAN), bounds_ref[0], jnp.float32)
    higher = jnp.full((1, SPAN), bounds_ref[1], jnp.float32)
    theta = (higher + lower) / 2
    delta = (higher - lower) / 2
    sigma = theta / delta
    rho = 1.0 / sigma

    def product(value, r, axis):
        high = value.astype(jnp.bfloat16)
        low = (value - high.astype(jnp.float32)).astype(jnp.bfloat16)
        dims = (((1,), (axis,)), ((), ()))

        def dot(a, b):
            return lax.dot_general(a, b, dims, preferred_element_type=jnp.float32)

        both = dot(jnp.concatenate([high, low], axis=0), high_ref[r])
        return both[:members] + (both[members:] + dot(high, low_ref[r]))

    for r in range(rows):
        dir_ref[r] = res_ref[r] / theta
        inc_ref[r] = dir_ref[r]
    for _ in range(ITERS):
        rho_next = 1.0 / (2 * sigma - rho)
        for r in range(rows):
            direction = dir_ref[r]
            middle = product(direction, r, 0) * inverse_ref[r : r + 1, :]
            applied = product(middle, r, 1) + inverse_ref[4 + r : 5 + r, :] * direction
            residue = res_ref[r] - applied
            direction = (rho_next * rho) * direction + (2 * rho_next / delta) * residue
            res_ref[r] = residue
            dir_ref[r] = direction
            inc_ref[r] = inc_ref[r] + direction
        rho = rho_next
    for r in range(rows):
        out_ref[pl.ds(r, blocks, stride=rows), :] = inc_ref[r, :, :blocks].T


def vmem(count):
    return [pl.BlockSpec(memory_space=pltpu.VMEM)] * count


def hbm(count):
    return [pl.BlockSpec(memory_space=pltpu.HBM)] * count


def pack(pred_back, ridge, ensemble, observed, obs_var):
    local_blocks, rows, members = ensemble.shape
    peers = rows // 4
    operands = [
        pltpu.with_memory_space_constraint(value, pltpu.HBM)
        for value in (pred_back, ridge, ensemble, observed, obs_var)
    ]
    return pl.pallas_call(
        pack_kernel,
        out_shape=pltpu.VMEM((peers * CHUNK, members), jnp.float32),
        in_specs=hbm(5),
        out_specs=vmem(1)[0],
        scratch_shapes=[
            pltpu.SMEM(pred_back.shape, jnp.int32),
            pltpu.SMEM(ridge.shape, jnp.float32),
            pltpu.VMEM(ensemble.shape, jnp.float32),
            pltpu.VMEM(observed.shape, jnp.float32),
            pltpu.VMEM(obs_var.shape, jnp.float32),
            pltpu.SemaphoreType.DMA((5,)),
        ],
        compiler_params=PARAMS,
        name="pack",
    )(*operands)


def local(own):
    members = own.shape[1]
    flat = jax.ShapeDtypeStruct((4, members, LANES), jnp.float32)
    return pl.pallas_call(
        local_kernel,
        out_shape=[
            flat,
            flat,
            jax.ShapeDtypeStruct((8, LANES), jnp.float32),
            jax.ShapeDtypeStruct((REACH + 1, 4, LANES), jnp.float32),
        ],
        in_specs=vmem(1),
        out_specs=vmem(4),
        scratch_shapes=[pltpu.VMEM((2, 4 * LANES, members), jnp.float32)],
        compiler_params=PARAMS,
        name="local",
    )(own)


def solve(bounds, own, first, second, mine):
    members, rows = own.shape[1], 4
    square = (rows, SPAN, SPAN)
    wide = pltpu.VMEM((rows, members, SPAN), jnp.float32)
    return pl.pallas_call(
        solve_kernel,
        out_shape=jax.ShapeDtypeStruct((own.shape[0] // CHUNK * 2 * rows, members), jnp.float32),
        in_specs=hbm(1) + vmem(7),
        out_specs=vmem(1)[0],
        scratch_shapes=[
            pltpu.VMEM((2, rows * LANES, members), jnp.float32),
            pltpu.VMEM((LANES, members), jnp.float32),
            wide,
            pltpu.VMEM(square, jnp.float32),
            pltpu.VMEM(square, jnp.bfloat16),
            pltpu.VMEM(square, jnp.bfloat16),
            pltpu.VMEM((8, SPAN), jnp.float32),
            pltpu.VMEM((REACH + 1, 8, LANES), jnp.float32),
            pltpu.VMEM((REACH, 8, LANES), jnp.float32),
            pltpu.VMEM((META, SPAN), jnp.float32),
            wide,
            wide,
            wide,
            pltpu.SMEM(bounds.shape, jnp.float32),
            pltpu.SemaphoreType.DMA,
        ],
        compiler_params=PARAMS,
        name="solve",
    )(pltpu.with_memory_space_constraint(bounds, pltpu.HBM), own, first, second, *mine)


def on_device(ensemble, observed, obs_var, ridge, pred_back, bounds):
    local_blocks, rows, members = ensemble.shape
    slots = pred_back.shape[1]
    region_blocks = lax.axis_size("blk") * local_blocks
    regions = lax.axis_size("region")
    per_device = rows // lax.axis_size("blk")
    assert (local_blocks, per_device, members, region_blocks) == (2, 4, LANES, LANES)
    groups = rows // 8
    peers = 2 * groups
    odd = (lax.axis_index("blk") & 1).astype(jnp.uint32)
    edge = HALO // local_blocks
    starts = [(1 - odd) * (peers - edge), odd * (peers - edge)]
    observed, *starts = lax.optimization_barrier((observed, *starts))
    packed = pack(pred_back, ridge, ensemble, observed, obs_var)
    own = lax.all_to_all(packed.reshape(peers, 1, CHUNK * members), "blk", 0, 0, tiled=True)
    flat = own.reshape(peers * CHUNK, members)
    mine = local(flat)
    halo = []
    for turn in range(2):
        pairs = []
        for region in range(regions):
            for place in range(peers):
                target = region + (1 if place % 2 == turn else -1)
                if 0 <= target < regions:
                    pairs.append((region * peers + place, target * peers + place))
        none = jnp.uint32(0)
        part = lax.dynamic_slice(own, (starts[turn], none, none), (edge, 1, own.shape[2]))
        part = lax.ppermute(part, AXES, pairs)
        halo.append(part.reshape(edge * CHUNK, members))
    increment = solve(bounds, flat, *halo, mine)
    increment = increment.reshape(2 * groups, local_blocks * per_device, members)
    increment = lax.all_to_all(increment, "blk", 0, 0, tiled=True)
    return pl.pallas_call(
        add_kernel,
        out_shape=jax.ShapeDtypeStruct(ensemble.shape, jnp.float32),
        in_specs=vmem(2),
        out_specs=vmem(1)[0],
        compiler_params=PARAMS,
        name="add",
    )(ensemble, increment.reshape(groups, 2, 8, members))


def solution(mesh):
    return jax.shard_map(
        on_device,
        mesh=mesh,
        in_specs=(
            P(AXES, None, None),
            P(AXES, None, None),
            P(AXES, None),
            P(AXES),
            P(AXES, None),
            P(),
        ),
        out_specs=P(AXES, None, None),
        check_vma=False,
    )
```

```python
import jax
import jax.numpy as jnp
from jax import lax
from jax.experimental import pallas as pl
from jax.experimental.pallas import tpu as pltpu
from jax.sharding import PartitionSpec as P

REACH = 16
ITERS = 3
HALO = ITERS * REACH
AXES = ("region", "blk")
LANES = 128
SPAN = 256
FIRST = 9
SECOND = 8
CHUNK = FIRST + SECOND
META = 16
HIGHEST = lax.Precision.HIGHEST
PARAMS = pltpu.CompilerParams(vmem_limit_bytes=48 * 1024 * 1024)


def iota(shape, axis):
    return lax.broadcasted_iota(jnp.int32, shape, axis)


def pack_kernel(
    pred_hbm, ridge_hbm, ens_hbm, obs_hbm, var_hbm, out_ref,
    pred_ref, ridge_ref, ens_ref, obs_ref, var_ref, sems,
):
    pairs = [
        (ens_hbm, ens_ref), (var_hbm, var_ref), (pred_hbm, pred_ref), (ridge_hbm, ridge_ref),
        (obs_hbm, obs_ref),
    ]
    copies = [pltpu.make_async_copy(a, b, sems.at[i]) for i, (a, b) in enumerate(pairs)]
    for copy in copies:
        copy.start()
    local_blocks, rows, members = ens_ref.shape
    slots = pred_ref.shape[1]
    last = members - 1
    groups = rows // 8
    low = iota((groups, 8, members), 1) < 4
    lane = iota((rows, members), 1)
    spot = iota((1, members), 1)

    def deal(blocks, start):
        blocks = [block.reshape(groups, 8, members) for block in blocks]
        even = jnp.where(low, blocks[0], pltpu.roll(blocks[1], 4, 1))
        odd = jnp.where(low, pltpu.roll(blocks[0], 4, 1), blocks[1])
        for q in range(groups):
            at = 2 * q * CHUNK + start
            out_ref[at : at + 8, :] = even[q]
            out_ref[at + CHUNK : at + CHUNK + 8, :] = odd[q]

    for copy in copies[:4]:
        copy.wait()
    meta = jnp.zeros((1, members), jnp.float32)
    blocks = []
    for b in range(local_blocks):
        for k in range(slots):
            meta = jnp.where(spot == META * b + k, pred_ref[b, k].astype(jnp.float32), meta)
        meta = jnp.where(spot == META * b + slots, ridge_ref[b], meta)
        ens = ens_ref[b]
        anomaly = (ens - jnp.mean(ens, axis=1, keepdims=True)) * (1.0 / (members - 1) ** 0.5)
        folded = anomaly + anomaly[:, last:] * (1.0 / (members**0.5 - 1.0))
        variance = jnp.broadcast_to(var_ref[b : b + 1, :], (members, rows)).T
        blocks.append(jnp.where(lane == last, variance, folded))
    deal(blocks, 0)
    for p in range(2 * groups):
        out_ref[p * CHUNK + FIRST - 1 : p * CHUNK + FIRST, :] = meta
    copies[4].wait()
    deal([obs_ref[b] - ens_ref[b] for b in range(local_blocks)], FIRST)


def add_kernel(ens_ref, inc_ref, out_ref):
    groups, _, _, members = inc_ref.shape
    low = iota((groups, 8, members), 1) < 4
    even, odd = inc_ref[:, 0], inc_ref[:, 1]
    shape = ens_ref.shape[1:]
    out_ref[0] = ens_ref[0] + jnp.where(low, even, pltpu.roll(odd, 4, 1)).reshape(shape)
    out_ref[1] = ens_ref[1] + jnp.where(low, pltpu.roll(even, 4, 1), odd).reshape(shape)


def solve_lags(gram, target):
    size = len(target)
    factor = {}
    inverse = []
    for j in range(size):
        for i in range(j, size):
            running = gram[i, j]
            for k in range(j):
                running = running - factor[i, k] * factor[j, k]
            if i == j:
                inverse.append(lax.rsqrt(running))
            else:
                factor[i, j] = running * inverse[j]
    forward = []
    for i in range(size):
        running = target[i]
        for k in range(i):
            running = running - factor[i, k] * forward[k]
        forward.append(running * inverse[i])
    beta = [None] * size
    for i in reversed(range(size)):
        running = forward[i]
        for k in range(i + 1, size):
            running = running - factor[k, i] * beta[k]
        beta[i] = running * inverse[i]
    return beta


def parity():
    return (lax.axis_index("blk") + lax.axis_index("region")) & 1


def lag_sums(x, sums_ref, row):
    for lag in range(REACH + 1):
        other = pltpu.roll(x, lag, 1) if lag else x
        sums_ref[lag, row : row + 1, :] = jnp.sum(x * other, axis=0, keepdims=True)


def line_up(ref, tile_ref, at, parts=(0, 1), first=0, count=None):
    for s in range(first, first + (count or ref.shape[0] // CHUNK)):
        for part in parts:
            row = s * CHUNK + (0, FIRST)[part]
            tile_ref[part, 8 * at : 8 * (at + 1), :] = ref[row : row + 8, :]
        at += 1


def columns(tile_ref, r, x_ref, res_ref, inverse_ref, lanes):
    members = LANES
    x = tile_ref[0, pl.ds(r, LANES, stride=4), :].T
    variance = x[members - 1 :, :]
    inverse = 1.0 / jnp.where(variance > 0, variance, 1.0)
    x = jnp.where(iota((members, LANES), 0) == members - 1, 0.0, x)
    x_ref[r, :, lanes] = x
    res_ref[r, :, lanes] = tile_ref[1, pl.ds(r, LANES, stride=4), :].T * inverse
    inverse_ref[4 + r : 5 + r, lanes] = inverse
    return x


def local_kernel(own_ref, x_ref, res_ref, inverse_ref, sums_ref, tile_ref):
    line_up(own_ref, tile_ref, 0)
    inverse_ref[0:4, :] = jnp.zeros((4, LANES), jnp.float32)
    for r in range(4):
        x = columns(tile_ref, r, x_ref, res_ref, inverse_ref, slice(0, LANES))
        lag_sums(x, sums_ref, r)


def solve_kernel(
    bounds_hbm, own_ref, first_ref, second_ref, own_x_ref, own_res_ref, own_inverse_ref, own_sums_ref,
    out_ref,
    tile_ref, fact_ref, x_ref, exact_ref, high_ref, low_ref, inverse_ref,
    sums_ref, beta_ref, meta_ref, res_ref, dir_ref, inc_ref, bounds_ref, sem,
):
    copy = pltpu.make_async_copy(bounds_hbm, bounds_ref, sem)
    copy.start()
    edge = first_ref.shape[0] // CHUNK
    peers = own_ref.shape[0] // CHUNK
    reach = REACH // 2
    after, before, head = reach, reach + edge, reach + 2 * edge

    def facts(ref):
        return ref[pl.ds(FIRST - 1, ref.shape[0] // CHUNK, stride=CHUNK), :]

    own_facts = facts(own_ref)
    fact_ref[0:peers, :] = own_facts
    fact_ref[peers : peers + reach, :] = own_facts[peers - reach :]
    fact_ref[peers + head :, :] = own_facts[:reach]
    line_up(own_ref, tile_ref, 0, (0,), peers - reach, reach)
    line_up(own_ref, tile_ref, head, (0,), 0, reach)
    for at in (0, head):
        tile_ref[1, 8 * at : 8 * (at + reach), :] = jnp.zeros((8 * reach, LANES), jnp.float32)
    for turn in range(2):

        @pl.when(parity() == turn)
        def _():
            for ref, at in (((first_ref, second_ref)[turn], after), ((second_ref, first_ref)[turn], before)):
                line_up(ref, tile_ref, at)
                fact_ref[peers + at : peers + at + edge, :] = facts(ref)

    for r in range(4):
        x_ref[r, :, :LANES] = own_x_ref[r]
        res_ref[r, :, :LANES] = own_res_ref[r]
    inverse_ref[:, :LANES] = own_inverse_ref[...]
    for r in range(4):
        x = columns(tile_ref, r, x_ref, res_ref, inverse_ref, slice(LANES, SPAN))
        lag_sums(x, sums_ref, 4 + r)
    sums_ref[:, 0:4, :] = own_sums_ref[...]
    regress(fact_ref, high_ref, low_ref, inverse_ref, x_ref, exact_ref, sums_ref, beta_ref, meta_ref)
    copy.wait()
    iterate(bounds_ref, high_ref, low_ref, inverse_ref, out_ref, res_ref, dir_ref, inc_ref)


def regress(fact_ref, high_ref, low_ref, inverse_ref, x_ref, exact_ref, sums_ref, beta_ref, meta_ref):
    rows = 4
    slots = 12
    facts = fact_ref[...].T
    spread = iota((LANES, SPAN), 1) - 2 * iota((LANES, SPAN), 0)
    meta_ref[...] = sum(
        jnp.dot(
            facts[META * b : META * (b + 1), :],
            jnp.where(spread == b, 1.0, 0.0),
            precision=HIGHEST,
            preferred_element_type=jnp.float32,
        )
        for b in range(2)
    )

    upper_half = iota((8, LANES), 0) >= 4
    lane = iota((8, LANES), 1)

    def packed(k):
        return jnp.where(upper_half, meta_ref[k : k + 1, LANES:], meta_ref[k : k + 1, :LANES])

    def crossed(value):
        return pltpu.roll(pltpu.roll(value, REACH, 1), 4, 0)

    edge_lane = lane < REACH
    sums = [sums_ref[lag] for lag in range(REACH + 1)]
    sums = [jnp.where(edge_lane, crossed(value), value) for value in sums]

    picks = [packed(k) for k in range(slots)]
    ridge = packed(slots)
    used = []
    for lag in range(1, REACH + 1):
        hit = jnp.abs(picks[0] - lag) < 0.5
        for k in range(1, slots):
            hit = hit | (jnp.abs(picks[k] - lag) < 0.5)
        used.append(jnp.where(hit, 1.0, 0.0))
    gram = {}
    for i in range(REACH):
        for j in range(i):
            gram[i, j] = pltpu.roll(sums[i - j], j + 1, 1) * (used[i] * used[j])
        gram[i, i] = jnp.where(used[i] > 0, pltpu.roll(sums[0], i + 1, 1) + ridge, 1.0)
    target = [sums[i + 1] * used[i] for i in range(REACH)]
    beta = solve_lags(gram, target)
    known = (lane >= REACH) & (lane < REACH + HALO)
    known = known | ((lane >= HALO + 2 * REACH) & (lane < REACH + 2 * HALO))
    for i in range(REACH):
        value = jnp.where(edge_lane & ~upper_half, crossed(beta[i]), beta[i])
        beta_ref[i] = jnp.where(upper_half & ~known, 0.0, -value)

    def fill(row, count, half, lag_of):
        for at in range(row, row + count, 16):
            part = lag_of[at - row : at - row + 16]
            factors = [jnp.where(part == 0, 1.0, 0.0)] * rows
            for lag in range(1, REACH + 1):
                hit = part == lag
                for r in range(rows):
                    value = beta_ref[lag - 1, 4 * half + r : 4 * half + r + 1, :]
                    factors[r] = jnp.where(hit, value, factors[r])
            store(at, 16, half, factors)

    def store(row, count, half, factors):
        lanes = slice(half * LANES, (half + 1) * LANES)
        for r in range(rows):
            high = factors[r].astype(jnp.bfloat16)
            low = (factors[r] - high.astype(jnp.float32)).astype(jnp.bfloat16)
            exact_ref[r, row : row + count, lanes] = factors[r]
            high_ref[r, row : row + count, lanes] = high
            low_ref[r, row : row + count, lanes] = low

    square = (LANES, LANES)
    row, column = iota(square, 0), iota(square, 1)
    lag_of = column - row
    fill(0, LANES, 0, lag_of)
    copied = (row < REACH) | (row >= LANES - REACH)
    fill(LANES, LANES, 1, jnp.where(copied & (lag_of != 0), -1, lag_of))
    corner = column[:REACH] - row[:REACH]
    fill(LANES - REACH, REACH, 1, jnp.where(corner == 0, -1, corner))
    before_end = REACH + 2 * HALO
    corner = column[:REACH] - row[:REACH] + REACH
    fill(LANES + before_end - REACH, REACH, 0, corner)
    for start, stop, half in (
        (0, LANES - REACH, 1),
        (LANES, LANES + before_end - REACH, 0),
        (LANES + before_end, SPAN, 0),
    ):
        store(start, stop - start, half, [jnp.zeros((stop - start, LANES), jnp.float32)] * rows)

    for r in range(rows):
        resid = jnp.dot(
            x_ref[r], exact_ref[r], precision=HIGHEST, preferred_element_type=jnp.float32
        )
        total = jnp.sum(resid * resid, axis=0, keepdims=True)
        inverse_ref[r : r + 1, :] = 1.0 / (total + 1e-05)


def iterate(bounds_ref, high_ref, low_ref, inverse_ref, out_ref, res_ref, dir_ref, inc_ref):
    rows = 4
    members = LANES
    blocks = out_ref.shape[0] // rows
    lower = jnp.full((1, SPAN), bounds_ref[0], jnp.float32)
    higher = jnp.full((1, SPAN), bounds_ref[1], jnp.float32)
    theta = (higher + lower) / 2
    delta = (higher - lower) / 2
    sigma = theta / delta
    rho = 1.0 / sigma

    def product(value, r, axis):
        high = value.astype(jnp.bfloat16)
        low = (value - high.astype(jnp.float32)).astype(jnp.bfloat16)
        dims = (((1,), (axis,)), ((), ()))

        def dot(a, b):
            return lax.dot_general(a, b, dims, preferred_element_type=jnp.float32)

        both = dot(jnp.concatenate([high, low], axis=0), high_ref[r])
        return both[:members] + (both[members:] + dot(high, low_ref[r]))

    for r in range(rows):
        dir_ref[r] = res_ref[r] / theta
        inc_ref[r] = dir_ref[r]
    for _ in range(ITERS):
        rho_next = 1.0 / (2 * sigma - rho)
        for r in range(rows):
            direction = dir_ref[r]
            middle = product(direction, r, 0) * inverse_ref[r : r + 1, :]
            applied = product(middle, r, 1) + inverse_ref[4 + r : 5 + r, :] * direction
            residue = res_ref[r] - applied
            direction = (rho_next * rho) * direction + (2 * rho_next / delta) * residue
            res_ref[r] = residue
            dir_ref[r] = direction
            inc_ref[r] = inc_ref[r] + direction
        rho = rho_next
    for r in range(rows):
        out_ref[pl.ds(r, blocks, stride=rows), :] = inc_ref[r, :, :blocks].T


def vmem(count):
    return [pl.BlockSpec(memory_space=pltpu.VMEM)] * count


def hbm(count):
    return [pl.BlockSpec(memory_space=pltpu.HBM)] * count


def pack(pred_back, ridge, ensemble, observed, obs_var):
    local_blocks, rows, members = ensemble.shape
    peers = rows // 4
    operands = [
        pltpu.with_memory_space_constraint(value, pltpu.HBM)
        for value in (pred_back, ridge, ensemble, observed, obs_var)
    ]
    return pl.pallas_call(
        pack_kernel,
        out_shape=pltpu.VMEM((peers * CHUNK, members), jnp.float32),
        in_specs=hbm(5),
        out_specs=vmem(1)[0],
        scratch_shapes=[
            pltpu.SMEM(pred_back.shape, jnp.int32),
            pltpu.SMEM(ridge.shape, jnp.float32),
            pltpu.VMEM(ensemble.shape, jnp.float32),
            pltpu.VMEM(observed.shape, jnp.float32),
            pltpu.VMEM(obs_var.shape, jnp.float32),
            pltpu.SemaphoreType.DMA((5,)),
        ],
        compiler_params=PARAMS,
        name="pack",
    )(*operands)


def local(own):
    members = own.shape[1]
    flat = jax.ShapeDtypeStruct((4, members, LANES), jnp.float32)
    return pl.pallas_call(
        local_kernel,
        out_shape=[
            flat,
            flat,
            jax.ShapeDtypeStruct((8, LANES), jnp.float32),
            jax.ShapeDtypeStruct((REACH + 1, 4, LANES), jnp.float32),
        ],
        in_specs=vmem(1),
        out_specs=vmem(4),
        scratch_shapes=[pltpu.VMEM((2, 4 * LANES, members), jnp.float32)],
        compiler_params=PARAMS,
        name="local",
    )(own)


def solve(bounds, own, first, second, mine):
    members, rows = own.shape[1], 4
    square = (rows, SPAN, SPAN)
    wide = pltpu.VMEM((rows, members, SPAN), jnp.float32)
    return pl.pallas_call(
        solve_kernel,
        out_shape=jax.ShapeDtypeStruct((own.shape[0] // CHUNK * 2 * rows, members), jnp.float32),
        in_specs=hbm(1) + vmem(7),
        out_specs=vmem(1)[0],
        scratch_shapes=[
            pltpu.VMEM((2, rows * LANES, members), jnp.float32),
            pltpu.VMEM((LANES, members), jnp.float32),
            wide,
            pltpu.VMEM(square, jnp.float32),
            pltpu.VMEM(square, jnp.bfloat16),
            pltpu.VMEM(square, jnp.bfloat16),
            pltpu.VMEM((8, SPAN), jnp.float32),
            pltpu.VMEM((REACH + 1, 8, LANES), jnp.float32),
            pltpu.VMEM((REACH, 8, LANES), jnp.float32),
            pltpu.VMEM((META, SPAN), jnp.float32),
            wide,
            wide,
            wide,
            pltpu.SMEM(bounds.shape, jnp.float32),
            pltpu.SemaphoreType.DMA,
        ],
        compiler_params=PARAMS,
        name="solve",
    )(pltpu.with_memory_space_constraint(bounds, pltpu.HBM), own, first, second, *mine)


def on_device(ensemble, observed, obs_var, ridge, pred_back, bounds):
    local_blocks, rows, members = ensemble.shape
    slots = pred_back.shape[1]
    region_blocks = lax.axis_size("blk") * local_blocks
    regions = lax.axis_size("region")
    per_device = rows // lax.axis_size("blk")
    assert (local_blocks, per_device, members, region_blocks) == (2, 4, LANES, LANES)
    groups = rows // 8
    peers = 2 * groups
    odd = parity().astype(jnp.uint32)
    edge = HALO // local_blocks
    starts = [(1 - odd) * (peers - edge), odd * (peers - edge)]
    observed, *starts = lax.optimization_barrier((observed, *starts))
    packed = pack(pred_back, ridge, ensemble, observed, obs_var)
    own = lax.all_to_all(packed.reshape(peers, 1, CHUNK * members), "blk", 0, 0, tiled=True)
    flat = own.reshape(peers * CHUNK, members)
    mine = local(flat)
    halo = []
    for turn in range(2):
        pairs = []
        for region in range(regions):
            for place in range(peers):
                target = region + (1 if (place + region) % 2 == turn else -1)
                if 0 <= target < regions:
                    pairs.append((region * peers + place, target * peers + place))
        none = jnp.uint32(0)
        part = lax.dynamic_slice(own, (starts[turn], none, none), (edge, 1, own.shape[2]))
        part = lax.ppermute(part, AXES, pairs)
        halo.append(part.reshape(edge * CHUNK, members))
    increment = solve(bounds, flat, *halo, mine)
    increment = increment.reshape(2 * groups, local_blocks * per_device, members)
    increment = lax.all_to_all(increment, "blk", 0, 0, tiled=True)
    return pl.pallas_call(
        add_kernel,
        out_shape=jax.ShapeDtypeStruct(ensemble.shape, jnp.float32),
        in_specs=vmem(2),
        out_specs=vmem(1)[0],
        compiler_params=PARAMS,
        name="add",
    )(ensemble, increment.reshape(groups, 2, 8, members))


def solution(mesh):
    return jax.shard_map(
        on_device,
        mesh=mesh,
        in_specs=(
            P(AXES, None, None),
            P(AXES, None, None),
            P(AXES, None),
            P(AXES),
            P(AXES, None),
            P(),
        ),
        out_specs=P(AXES, None, None),
        check_vma=False,
    )
```

```python
import jax
import jax.numpy as jnp
from jax import lax
from jax.experimental import pallas as pl
from jax.experimental.pallas import tpu as pltpu
from jax.sharding import PartitionSpec as P

REACH = 16
ITERS = 3
HALO = ITERS * REACH
AXES = ("region", "blk")
LANES = 128
SPAN = 256
FIRST = 9
SECOND = 8
CHUNK = FIRST + SECOND
META = 16
HIGHEST = lax.Precision.HIGHEST
PARAMS = pltpu.CompilerParams(vmem_limit_bytes=48 * 1024 * 1024)


def iota(shape, axis):
    return lax.broadcasted_iota(jnp.int32, shape, axis)


def pack_kernel(
    pred_hbm, ridge_hbm, ens_hbm, obs_hbm, var_hbm, out_ref,
    pred_ref, ridge_ref, ens_ref, obs_ref, var_ref, sems,
):
    pairs = [
        (ens_hbm, ens_ref), (var_hbm, var_ref), (pred_hbm, pred_ref), (ridge_hbm, ridge_ref),
        (obs_hbm, obs_ref),
    ]
    copies = [pltpu.make_async_copy(a, b, sems.at[i]) for i, (a, b) in enumerate(pairs)]
    for copy in copies:
        copy.start()
    local_blocks, rows, members = ens_ref.shape
    slots = pred_ref.shape[1]
    last = members - 1
    groups = rows // 8
    low = iota((groups, 8, members), 1) < 4
    lane = iota((rows, members), 1)
    spot = iota((1, members), 1)

    def deal(blocks, start):
        blocks = [block.reshape(groups, 8, members) for block in blocks]
        even = jnp.where(low, blocks[0], pltpu.roll(blocks[1], 4, 1))
        odd = jnp.where(low, pltpu.roll(blocks[0], 4, 1), blocks[1])
        for q in range(groups):
            at = 2 * q * CHUNK + start
            out_ref[at : at + 8, :] = even[q]
            out_ref[at + CHUNK : at + CHUNK + 8, :] = odd[q]

    for copy in copies[:4]:
        copy.wait()
    meta = jnp.zeros((1, members), jnp.float32)
    blocks = []
    for b in range(local_blocks):
        for k in range(slots):
            meta = jnp.where(spot == META * b + k, pred_ref[b, k].astype(jnp.float32), meta)
        meta = jnp.where(spot == META * b + slots, ridge_ref[b], meta)
        ens = ens_ref[b]
        anomaly = (ens - jnp.mean(ens, axis=1, keepdims=True)) * (1.0 / (members - 1) ** 0.5)
        folded = anomaly + anomaly[:, last:] * (1.0 / (members**0.5 - 1.0))
        variance = jnp.broadcast_to(var_ref[b : b + 1, :], (members, rows)).T
        blocks.append(jnp.where(lane == last, variance, folded))
    deal(blocks, 0)
    for p in range(2 * groups):
        out_ref[p * CHUNK + FIRST - 1 : p * CHUNK + FIRST, :] = meta
    copies[4].wait()
    deal([obs_ref[b] - ens_ref[b] for b in range(local_blocks)], FIRST)


def add_kernel(ens_ref, inc_ref, out_ref):
    groups, _, _, members = inc_ref.shape
    low = iota((groups, 8, members), 1) < 4
    even, odd = inc_ref[:, 0], inc_ref[:, 1]
    shape = ens_ref.shape[1:]
    out_ref[0] = ens_ref[0] + jnp.where(low, even, pltpu.roll(odd, 4, 1)).reshape(shape)
    out_ref[1] = ens_ref[1] + jnp.where(low, pltpu.roll(even, 4, 1), odd).reshape(shape)


def solve_lags(gram, target):
    size = len(target)
    factor = {}
    inverse = []
    for j in range(size):
        for i in range(j, size):
            running = gram[i, j]
            for k in range(j):
                running = running - factor[i, k] * factor[j, k]
            if i == j:
                inverse.append(lax.rsqrt(running))
            else:
                factor[i, j] = running * inverse[j]
    forward = []
    for i in range(size):
        running = target[i]
        for k in range(i):
            running = running - factor[i, k] * forward[k]
        forward.append(running * inverse[i])
    beta = [None] * size
    for i in reversed(range(size)):
        running = forward[i]
        for k in range(i + 1, size):
            running = running - factor[k, i] * beta[k]
        beta[i] = running * inverse[i]
    return beta


def parity():
    return lax.axis_index("blk") % 2


def lag_sums(x, sums_ref, row):
    for lag in range(REACH + 1):
        other = pltpu.roll(x, lag, 1) if lag else x
        sums_ref[lag, row : row + 1, :] = jnp.sum(x * other, axis=0, keepdims=True)


def line_up(ref, tile_ref, at, parts=(0, 1), first=0, count=None):
    for s in range(first, first + (count or ref.shape[0] // CHUNK)):
        for part in parts:
            row = s * CHUNK + (0, FIRST)[part]
            tile_ref[part, 8 * at : 8 * (at + 1), :] = ref[row : row + 8, :]
        at += 1


def columns(tile_ref, r, x_ref, res_ref, inverse_ref, lanes):
    members = LANES
    x = tile_ref[0, pl.ds(r, LANES, stride=4), :].T
    variance = x[members - 1 :, :]
    inverse = 1.0 / jnp.where(variance > 0, variance, 1.0)
    x = jnp.where(iota((members, LANES), 0) == members - 1, 0.0, x)
    x_ref[r, :, lanes] = x
    res_ref[r, :, lanes] = tile_ref[1, pl.ds(r, LANES, stride=4), :].T * inverse
    inverse_ref[4 + r : 5 + r, lanes] = inverse
    return x


def local_kernel(own_ref, x_ref, res_ref, inverse_ref, sums_ref, tile_ref):
    line_up(own_ref, tile_ref, 0)
    inverse_ref[0:4, :] = jnp.zeros((4, LANES), jnp.float32)
    for r in range(4):
        x = columns(tile_ref, r, x_ref, res_ref, inverse_ref, slice(0, LANES))
        lag_sums(x, sums_ref, r)


def solve_kernel(
    bounds_hbm, own_ref, third_ref, second_ref, first_ref, own_x_ref, own_res_ref, own_inverse_ref, own_sums_ref,
    out_ref,
    tile_ref, fact_ref, x_ref, exact_ref, high_ref, low_ref, inverse_ref,
    sums_ref, beta_ref, meta_ref, res_ref, dir_ref, inc_ref, bounds_ref, sem,
):
    copy = pltpu.make_async_copy(bounds_hbm, bounds_ref, sem)
    copy.start()
    halo_refs = (first_ref, second_ref, third_ref)
    edge = first_ref.shape[0] // CHUNK
    peers = own_ref.shape[0] // CHUNK
    reach = REACH // 2
    after, before, head = reach, reach + edge, reach + 2 * edge

    def facts(ref):
        return ref[pl.ds(FIRST - 1, ref.shape[0] // CHUNK, stride=CHUNK), :]

    own_facts = facts(own_ref)
    fact_ref[0:peers, :] = own_facts
    fact_ref[peers : peers + reach, :] = own_facts[peers - reach :]
    fact_ref[peers + head :, :] = own_facts[:reach]
    line_up(own_ref, tile_ref, 0, (0,), peers - reach, reach)
    line_up(own_ref, tile_ref, head, (0,), 0, reach)
    for at in (0, head):
        tile_ref[1, 8 * at : 8 * (at + reach), :] = jnp.zeros((8 * reach, LANES), jnp.float32)
    for turn in range(2):

        @pl.when(parity() == turn)
        def _():
            for ref, at in ((halo_refs[turn], after), (halo_refs[turn + 1], before)):
                line_up(ref, tile_ref, at)
                fact_ref[peers + at : peers + at + edge, :] = facts(ref)

    for r in range(4):
        x_ref[r, :, :LANES] = own_x_ref[r]
        res_ref[r, :, :LANES] = own_res_ref[r]
    inverse_ref[:, :LANES] = own_inverse_ref[...]
    for r in range(4):
        x = columns(tile_ref, r, x_ref, res_ref, inverse_ref, slice(LANES, SPAN))
        lag_sums(x, sums_ref, 4 + r)
    sums_ref[:, 0:4, :] = own_sums_ref[...]
    regress(fact_ref, high_ref, low_ref, inverse_ref, x_ref, exact_ref, sums_ref, beta_ref, meta_ref)
    copy.wait()
    iterate(bounds_ref, high_ref, low_ref, inverse_ref, out_ref, res_ref, dir_ref, inc_ref)


def regress(fact_ref, high_ref, low_ref, inverse_ref, x_ref, exact_ref, sums_ref, beta_ref, meta_ref):
    rows = 4
    slots = 12
    facts = fact_ref[...].T
    spread = iota((LANES, SPAN), 1) - 2 * iota((LANES, SPAN), 0)
    meta_ref[...] = sum(
        jnp.dot(
            facts[META * b : META * (b + 1), :],
            jnp.where(spread == b, 1.0, 0.0),
            precision=HIGHEST,
            preferred_element_type=jnp.float32,
        )
        for b in range(2)
    )

    upper_half = iota((8, LANES), 0) >= 4
    lane = iota((8, LANES), 1)

    def packed(k):
        return jnp.where(upper_half, meta_ref[k : k + 1, LANES:], meta_ref[k : k + 1, :LANES])

    def crossed(value):
        return pltpu.roll(pltpu.roll(value, REACH, 1), 4, 0)

    edge_lane = lane < REACH
    sums = [sums_ref[lag] for lag in range(REACH + 1)]
    sums = [jnp.where(edge_lane, crossed(value), value) for value in sums]

    picks = [packed(k) for k in range(slots)]
    ridge = packed(slots)
    used = []
    for lag in range(1, REACH + 1):
        hit = jnp.abs(picks[0] - lag) < 0.5
        for k in range(1, slots):
            hit = hit | (jnp.abs(picks[k] - lag) < 0.5)
        used.append(jnp.where(hit, 1.0, 0.0))
    gram = {}
    for i in range(REACH):
        for j in range(i):
            gram[i, j] = pltpu.roll(sums[i - j], j + 1, 1) * (used[i] * used[j])
        gram[i, i] = jnp.where(used[i] > 0, pltpu.roll(sums[0], i + 1, 1) + ridge, 1.0)
    target = [sums[i + 1] * used[i] for i in range(REACH)]
    beta = solve_lags(gram, target)
    known = (lane >= REACH) & (lane < REACH + HALO)
    known = known | ((lane >= HALO + 2 * REACH) & (lane < REACH + 2 * HALO))
    for i in range(REACH):
        value = jnp.where(edge_lane & ~upper_half, crossed(beta[i]), beta[i])
        beta_ref[i] = jnp.where(upper_half & ~known, 0.0, -value)

    def fill(row, count, half, lag_of):
        for at in range(row, row + count, 16):
            part = lag_of[at - row : at - row + 16]
            factors = [jnp.where(part == 0, 1.0, 0.0)] * rows
            for lag in range(1, REACH + 1):
                hit = part == lag
                for r in range(rows):
                    value = beta_ref[lag - 1, 4 * half + r : 4 * half + r + 1, :]
                    factors[r] = jnp.where(hit, value, factors[r])
            store(at, 16, half, factors)

    def store(row, count, half, factors):
        lanes = slice(half * LANES, (half + 1) * LANES)
        for r in range(rows):
            high = factors[r].astype(jnp.bfloat16)
            low = (factors[r] - high.astype(jnp.float32)).astype(jnp.bfloat16)
            exact_ref[r, row : row + count, lanes] = factors[r]
            high_ref[r, row : row + count, lanes] = high
            low_ref[r, row : row + count, lanes] = low

    square = (LANES, LANES)
    row, column = iota(square, 0), iota(square, 1)
    lag_of = column - row
    fill(0, LANES, 0, lag_of)
    copied = (row < REACH) | (row >= LANES - REACH)
    fill(LANES, LANES, 1, jnp.where(copied & (lag_of != 0), -1, lag_of))
    corner = column[:REACH] - row[:REACH]
    fill(LANES - REACH, REACH, 1, jnp.where(corner == 0, -1, corner))
    before_end = REACH + 2 * HALO
    corner = column[:REACH] - row[:REACH] + REACH
    fill(LANES + before_end - REACH, REACH, 0, corner)
    for start, stop, half in (
        (0, LANES - REACH, 1),
        (LANES, LANES + before_end - REACH, 0),
        (LANES + before_end, SPAN, 0),
    ):
        store(start, stop - start, half, [jnp.zeros((stop - start, LANES), jnp.float32)] * rows)

    for r in range(rows):
        resid = jnp.dot(
            x_ref[r], exact_ref[r], precision=HIGHEST, preferred_element_type=jnp.float32
        )
        total = jnp.sum(resid * resid, axis=0, keepdims=True)
        inverse_ref[r : r + 1, :] = 1.0 / (total + 1e-05)


def iterate(bounds_ref, high_ref, low_ref, inverse_ref, out_ref, res_ref, dir_ref, inc_ref):
    rows = 4
    members = LANES
    blocks = out_ref.shape[0] // rows
    lower = jnp.full((1, SPAN), bounds_ref[0], jnp.float32)
    higher = jnp.full((1, SPAN), bounds_ref[1], jnp.float32)
    theta = (higher + lower) / 2
    delta = (higher - lower) / 2
    sigma = theta / delta
    rho = 1.0 / sigma

    def product(value, r, axis):
        high = value.astype(jnp.bfloat16)
        low = (value - high.astype(jnp.float32)).astype(jnp.bfloat16)
        dims = (((1,), (axis,)), ((), ()))

        def dot(a, b):
            return lax.dot_general(a, b, dims, preferred_element_type=jnp.float32)

        both = dot(jnp.concatenate([high, low], axis=0), high_ref[r])
        return both[:members] + (both[members:] + dot(high, low_ref[r]))

    for r in range(rows):
        dir_ref[r] = res_ref[r] / theta
        inc_ref[r] = dir_ref[r]
    for _ in range(ITERS):
        rho_next = 1.0 / (2 * sigma - rho)
        for r in range(rows):
            direction = dir_ref[r]
            middle = product(direction, r, 0) * inverse_ref[r : r + 1, :]
            applied = product(middle, r, 1) + inverse_ref[4 + r : 5 + r, :] * direction
            residue = res_ref[r] - applied
            direction = (rho_next * rho) * direction + (2 * rho_next / delta) * residue
            res_ref[r] = residue
            dir_ref[r] = direction
            inc_ref[r] = inc_ref[r] + direction
        rho = rho_next
    for r in range(rows):
        out_ref[pl.ds(r, blocks, stride=rows), :] = inc_ref[r, :, :blocks].T


def vmem(count):
    return [pl.BlockSpec(memory_space=pltpu.VMEM)] * count


def hbm(count):
    return [pl.BlockSpec(memory_space=pltpu.HBM)] * count


def pack(pred_back, ridge, ensemble, observed, obs_var):
    local_blocks, rows, members = ensemble.shape
    peers = rows // 4
    operands = [
        pltpu.with_memory_space_constraint(value, pltpu.HBM)
        for value in (pred_back, ridge, ensemble, observed, obs_var)
    ]
    return pl.pallas_call(
        pack_kernel,
        out_shape=pltpu.VMEM((peers * CHUNK, members), jnp.float32),
        in_specs=hbm(5),
        out_specs=vmem(1)[0],
        scratch_shapes=[
            pltpu.SMEM(pred_back.shape, jnp.int32),
            pltpu.SMEM(ridge.shape, jnp.float32),
            pltpu.VMEM(ensemble.shape, jnp.float32),
            pltpu.VMEM(observed.shape, jnp.float32),
            pltpu.VMEM(obs_var.shape, jnp.float32),
            pltpu.SemaphoreType.DMA((5,)),
        ],
        compiler_params=PARAMS,
        name="pack",
    )(*operands)


def local(own):
    members = own.shape[1]
    flat = jax.ShapeDtypeStruct((4, members, LANES), jnp.float32)
    return pl.pallas_call(
        local_kernel,
        out_shape=[
            flat,
            flat,
            jax.ShapeDtypeStruct((8, LANES), jnp.float32),
            jax.ShapeDtypeStruct((REACH + 1, 4, LANES), jnp.float32),
        ],
        in_specs=vmem(1),
        out_specs=vmem(4),
        scratch_shapes=[pltpu.VMEM((2, 4 * LANES, members), jnp.float32)],
        compiler_params=PARAMS,
        name="local",
    )(own)


def solve(bounds, own, halo, mine):
    members, rows = own.shape[1], 4
    square = (rows, SPAN, SPAN)
    wide = pltpu.VMEM((rows, members, SPAN), jnp.float32)
    return pl.pallas_call(
        solve_kernel,
        out_shape=jax.ShapeDtypeStruct((own.shape[0] // CHUNK * 2 * rows, members), jnp.float32),
        in_specs=hbm(1) + vmem(8),
        out_specs=vmem(1)[0],
        scratch_shapes=[
            pltpu.VMEM((2, rows * LANES, members), jnp.float32),
            pltpu.VMEM((LANES, members), jnp.float32),
            wide,
            pltpu.VMEM(square, jnp.float32),
            pltpu.VMEM(square, jnp.bfloat16),
            pltpu.VMEM(square, jnp.bfloat16),
            pltpu.VMEM((8, SPAN), jnp.float32),
            pltpu.VMEM((REACH + 1, 8, LANES), jnp.float32),
            pltpu.VMEM((REACH, 8, LANES), jnp.float32),
            pltpu.VMEM((META, SPAN), jnp.float32),
            wide,
            wide,
            wide,
            pltpu.SMEM(bounds.shape, jnp.float32),
            pltpu.SemaphoreType.DMA,
        ],
        compiler_params=PARAMS,
        name="solve",
    )(pltpu.with_memory_space_constraint(bounds, pltpu.HBM), own, *halo[::-1], *mine)


def on_device(ensemble, observed, obs_var, ridge, pred_back, bounds):
    local_blocks, rows, members = ensemble.shape
    slots = pred_back.shape[1]
    region_blocks = lax.axis_size("blk") * local_blocks
    regions = lax.axis_size("region")
    per_device = rows // lax.axis_size("blk")
    assert (local_blocks, per_device, members, region_blocks) == (2, 4, LANES, LANES)
    groups = rows // 8
    peers = 2 * groups
    odd = (lax.axis_index("blk") & 1).astype(jnp.uint32)
    edge = HALO // local_blocks
    start = (1 - odd) * (peers - edge)
    observed, start = lax.optimization_barrier((observed, start))
    packed = pack(pred_back, ridge, ensemble, observed, obs_var)
    own = lax.all_to_all(packed.reshape(peers, 1, CHUNK * members), "blk", 0, 0, tiled=True)
    flat = own.reshape(peers * CHUNK, members)
    mine = local(flat)

    def pairs(core, step):
        return [
            (region * peers + place, (region + step) * peers + place)
            for region in range(regions)
            for place in range(core, peers, 2)
            if 0 <= region + step < regions
        ]

    none = jnp.uint32(0)
    middle = lax.dynamic_slice(own, (start, none, none), (edge, 1, own.shape[2]))
    first = lax.ppermute(own[:edge], AXES, pairs(0, -1))
    second = lax.ppermute(middle, AXES, pairs(1, -1) + pairs(0, 1))
    third = lax.ppermute(own[peers - edge :], AXES, pairs(1, 1))
    halo = [part.reshape(edge * CHUNK, members) for part in (first, second, third)]
    increment = solve(bounds, flat, halo, mine)
    increment = increment.reshape(2 * groups, local_blocks * per_device, members)
    increment = lax.all_to_all(increment, "blk", 0, 0, tiled=True)
    return pl.pallas_call(
        add_kernel,
        out_shape=jax.ShapeDtypeStruct(ensemble.shape, jnp.float32),
        in_specs=vmem(2),
        out_specs=vmem(1)[0],
        compiler_params=PARAMS,
        name="add",
    )(ensemble, increment.reshape(groups, 2, 8, members))


def solution(mesh):
    return jax.shard_map(
        on_device,
        mesh=mesh,
        in_specs=(
            P(AXES, None, None),
            P(AXES, None, None),
            P(AXES, None),
            P(AXES),
            P(AXES, None),
            P(),
        ),
        out_specs=P(AXES, None, None),
        check_vma=False,
    )
```

```python
import jax
import jax.numpy as jnp
from jax import lax
from jax.experimental import pallas as pl
from jax.experimental.pallas import tpu as pltpu
from jax.sharding import PartitionSpec as P

REACH = 16
ITERS = 3
HALO = ITERS * REACH
AXES = ("region", "blk")
LANES = 128
SPAN = 256
FIRST = 9
SECOND = 8
CHUNK = FIRST + SECOND
META = 16
HIGHEST = lax.Precision.HIGHEST
PARAMS = pltpu.CompilerParams(vmem_limit_bytes=48 * 1024 * 1024)


def iota(shape, axis):
    return lax.broadcasted_iota(jnp.int32, shape, axis)


def pack_kernel(
    pred_hbm, ridge_hbm, ens_hbm, obs_hbm, var_hbm, out_ref,
    pred_ref, ridge_ref, ens_ref, obs_ref, var_ref, sems,
):
    pairs = [
        (ens_hbm.at[0], ens_ref.at[0]), (var_hbm, var_ref), (pred_hbm, pred_ref), (ridge_hbm, ridge_ref),
        (ens_hbm.at[1], ens_ref.at[1]), (obs_hbm, obs_ref),
    ]
    copies = [pltpu.make_async_copy(a, b, sems.at[i]) for i, (a, b) in enumerate(pairs)]
    for copy in copies:
        copy.start()
    local_blocks, rows, members = ens_ref.shape
    slots = pred_ref.shape[1]
    last = members - 1
    groups = rows // 8
    low = iota((groups, 8, members), 1) < 4
    lane = iota((rows, members), 1)
    spot = iota((1, members), 1)

    def deal(blocks, start):
        blocks = [block.reshape(groups, 8, members) for block in blocks]
        even = jnp.where(low, blocks[0], pltpu.roll(blocks[1], 4, 1))
        odd = jnp.where(low, pltpu.roll(blocks[0], 4, 1), blocks[1])
        for q in range(groups):
            at = 2 * q * CHUNK + start
            out_ref[at : at + 8, :] = even[q]
            out_ref[at + CHUNK : at + CHUNK + 8, :] = odd[q]

    for copy in copies[:4]:
        copy.wait()
    meta = jnp.zeros((1, members), jnp.float32)
    blocks = []
    for b in range(local_blocks):
        for k in range(slots):
            meta = jnp.where(spot == META * b + k, pred_ref[b, k].astype(jnp.float32), meta)
        meta = jnp.where(spot == META * b + slots, ridge_ref[b], meta)
        if b == 1:
            copies[4].wait()
        ens = ens_ref[b]
        anomaly = (ens - jnp.mean(ens, axis=1, keepdims=True)) * (1.0 / (members - 1) ** 0.5)
        folded = anomaly + anomaly[:, last:] * (1.0 / (members**0.5 - 1.0))
        variance = jnp.broadcast_to(var_ref[b : b + 1, :], (members, rows)).T
        blocks.append(jnp.where(lane == last, variance, folded))
    deal(blocks, 0)
    for p in range(2 * groups):
        out_ref[p * CHUNK + FIRST - 1 : p * CHUNK + FIRST, :] = meta
    copies[5].wait()
    deal([obs_ref[b] - ens_ref[b] for b in range(local_blocks)], FIRST)


def add_kernel(ens_ref, inc_ref, out_ref):
    groups, _, _, members = inc_ref.shape
    low = iota((groups, 8, members), 1) < 4
    even, odd = inc_ref[:, 0], inc_ref[:, 1]
    shape = ens_ref.shape[1:]
    out_ref[0] = ens_ref[0] + jnp.where(low, even, pltpu.roll(odd, 4, 1)).reshape(shape)
    out_ref[1] = ens_ref[1] + jnp.where(low, pltpu.roll(even, 4, 1), odd).reshape(shape)


def solve_lags(gram, target):
    size = len(target)
    factor = {}
    inverse = []
    for j in range(size):
        for i in range(j, size):
            running = gram[i, j]
            for k in range(j):
                running = running - factor[i, k] * factor[j, k]
            if i == j:
                inverse.append(lax.rsqrt(running))
            else:
                factor[i, j] = running * inverse[j]
    forward = []
    for i in range(size):
        running = target[i]
        for k in range(i):
            running = running - factor[i, k] * forward[k]
        forward.append(running * inverse[i])
    beta = [None] * size
    for i in reversed(range(size)):
        running = forward[i]
        for k in range(i + 1, size):
            running = running - factor[k, i] * beta[k]
        beta[i] = running * inverse[i]
    return beta


def parity():
    return lax.axis_index("blk") % 2


def lag_sums(x, sums_ref, row):
    for lag in range(REACH + 1):
        other = pltpu.roll(x, lag, 1) if lag else x
        sums_ref[lag, row : row + 1, :] = jnp.sum(x * other, axis=0, keepdims=True)


def line_up(ref, tile_ref, at, parts=(0, 1), first=0, count=None):
    for s in range(first, first + (count or ref.shape[0] // CHUNK)):
        for part in parts:
            row = s * CHUNK + (0, FIRST)[part]
            tile_ref[part, 8 * at : 8 * (at + 1), :] = ref[row : row + 8, :]
        at += 1


def columns(tile_ref, r, x_ref, res_ref, inverse_ref, lanes):
    members = LANES
    x = tile_ref[0, pl.ds(r, LANES, stride=4), :].T
    variance = x[members - 1 :, :]
    inverse = 1.0 / jnp.where(variance > 0, variance, 1.0)
    x = jnp.where(iota((members, LANES), 0) == members - 1, 0.0, x)
    x_ref[r, :, lanes] = x
    res_ref[r, :, lanes] = tile_ref[1, pl.ds(r, LANES, stride=4), :].T * inverse
    inverse_ref[4 + r : 5 + r, lanes] = inverse
    return x


def local_kernel(own_ref, x_ref, res_ref, inverse_ref, sums_ref, tile_ref):
    line_up(own_ref, tile_ref, 0)
    inverse_ref[0:4, :] = jnp.zeros((4, LANES), jnp.float32)
    for r in range(4):
        x = columns(tile_ref, r, x_ref, res_ref, inverse_ref, slice(0, LANES))
        lag_sums(x, sums_ref, r)


def solve_kernel(
    bounds_hbm, own_ref, third_ref, second_ref, first_ref, own_x_ref, own_res_ref, own_inverse_ref, own_sums_ref,
    out_ref,
    tile_ref, fact_ref, x_ref, exact_ref, high_ref, low_ref, inverse_ref,
    sums_ref, beta_ref, meta_ref, res_ref, dir_ref, inc_ref, bounds_ref, sem,
):
    copy = pltpu.make_async_copy(bounds_hbm, bounds_ref, sem)
    copy.start()
    halo_refs = (first_ref, second_ref, third_ref)
    edge = first_ref.shape[0] // CHUNK
    peers = own_ref.shape[0] // CHUNK
    reach = REACH // 2
    after, before, head = reach, reach + edge, reach + 2 * edge

    def facts(ref):
        return ref[pl.ds(FIRST - 1, ref.shape[0] // CHUNK, stride=CHUNK), :]

    own_facts = facts(own_ref)
    fact_ref[0:peers, :] = own_facts
    fact_ref[peers : peers + reach, :] = own_facts[peers - reach :]
    fact_ref[peers + head :, :] = own_facts[:reach]
    line_up(own_ref, tile_ref, 0, (0,), peers - reach, reach)
    line_up(own_ref, tile_ref, head, (0,), 0, reach)
    for at in (0, head):
        tile_ref[1, 8 * at : 8 * (at + reach), :] = jnp.zeros((8 * reach, LANES), jnp.float32)
    for turn in range(2):

        @pl.when(parity() == turn)
        def _():
            for ref, at in ((halo_refs[turn], after), (halo_refs[turn + 1], before)):
                line_up(ref, tile_ref, at)
                fact_ref[peers + at : peers + at + edge, :] = facts(ref)

    for r in range(4):
        x_ref[r, :, :LANES] = own_x_ref[r]
        res_ref[r, :, :LANES] = own_res_ref[r]
    inverse_ref[:, :LANES] = own_inverse_ref[...]
    for r in range(4):
        x = columns(tile_ref, r, x_ref, res_ref, inverse_ref, slice(LANES, SPAN))
        lag_sums(x, sums_ref, 4 + r)
    sums_ref[:, 0:4, :] = own_sums_ref[...]
    regress(fact_ref, high_ref, low_ref, inverse_ref, x_ref, exact_ref, sums_ref, beta_ref, meta_ref)
    copy.wait()
    iterate(bounds_ref, high_ref, low_ref, inverse_ref, out_ref, res_ref, dir_ref, inc_ref)


def regress(fact_ref, high_ref, low_ref, inverse_ref, x_ref, exact_ref, sums_ref, beta_ref, meta_ref):
    rows = 4
    slots = 12
    facts = fact_ref[...].T
    spread = iota((LANES, SPAN), 1) - 2 * iota((LANES, SPAN), 0)
    meta_ref[...] = sum(
        jnp.dot(
            facts[META * b : META * (b + 1), :],
            jnp.where(spread == b, 1.0, 0.0),
            precision=HIGHEST,
            preferred_element_type=jnp.float32,
        )
        for b in range(2)
    )

    upper_half = iota((8, LANES), 0) >= 4
    lane = iota((8, LANES), 1)

    def packed(k):
        return jnp.where(upper_half, meta_ref[k : k + 1, LANES:], meta_ref[k : k + 1, :LANES])

    def crossed(value):
        return pltpu.roll(pltpu.roll(value, REACH, 1), 4, 0)

    edge_lane = lane < REACH
    sums = [sums_ref[lag] for lag in range(REACH + 1)]
    sums = [jnp.where(edge_lane, crossed(value), value) for value in sums]

    picks = [packed(k) for k in range(slots)]
    ridge = packed(slots)
    used = []
    for lag in range(1, REACH + 1):
        hit = jnp.abs(picks[0] - lag) < 0.5
        for k in range(1, slots):
            hit = hit | (jnp.abs(picks[k] - lag) < 0.5)
        used.append(jnp.where(hit, 1.0, 0.0))
    gram = {}
    for i in range(REACH):
        for j in range(i):
            gram[i, j] = pltpu.roll(sums[i - j], j + 1, 1) * (used[i] * used[j])
        gram[i, i] = jnp.where(used[i] > 0, pltpu.roll(sums[0], i + 1, 1) + ridge, 1.0)
    target = [sums[i + 1] * used[i] for i in range(REACH)]
    beta = solve_lags(gram, target)
    known = (lane >= REACH) & (lane < REACH + HALO)
    known = known | ((lane >= HALO + 2 * REACH) & (lane < REACH + 2 * HALO))
    for i in range(REACH):
        value = jnp.where(edge_lane & ~upper_half, crossed(beta[i]), beta[i])
        beta_ref[i] = jnp.where(upper_half & ~known, 0.0, -value)

    def fill(row, count, half, lag_of):
        for at in range(row, row + count, 16):
            part = lag_of[at - row : at - row + 16]
            factors = [jnp.where(part == 0, 1.0, 0.0)] * rows
            for lag in range(1, REACH + 1):
                hit = part == lag
                for r in range(rows):
                    value = beta_ref[lag - 1, 4 * half + r : 4 * half + r + 1, :]
                    factors[r] = jnp.where(hit, value, factors[r])
            store(at, 16, half, factors)

    def store(row, count, half, factors):
        lanes = slice(half * LANES, (half + 1) * LANES)
        for r in range(rows):
            high = factors[r].astype(jnp.bfloat16)
            low = (factors[r] - high.astype(jnp.float32)).astype(jnp.bfloat16)
            exact_ref[r, row : row + count, lanes] = factors[r]
            high_ref[r, row : row + count, lanes] = high
            low_ref[r, row : row + count, lanes] = low

    square = (LANES, LANES)
    row, column = iota(square, 0), iota(square, 1)
    lag_of = column - row
    fill(0, LANES, 0, lag_of)
    copied = (row < REACH) | (row >= LANES - REACH)
    fill(LANES, LANES, 1, jnp.where(copied & (lag_of != 0), -1, lag_of))
    corner = column[:REACH] - row[:REACH]
    fill(LANES - REACH, REACH, 1, jnp.where(corner == 0, -1, corner))
    before_end = REACH + 2 * HALO
    corner = column[:REACH] - row[:REACH] + REACH
    fill(LANES + before_end - REACH, REACH, 0, corner)
    for start, stop, half in (
        (0, LANES - REACH, 1),
        (LANES, LANES + before_end - REACH, 0),
        (LANES + before_end, SPAN, 0),
    ):
        store(start, stop - start, half, [jnp.zeros((stop - start, LANES), jnp.float32)] * rows)

    for r in range(rows):
        resid = jnp.dot(
            x_ref[r], exact_ref[r], precision=HIGHEST, preferred_element_type=jnp.float32
        )
        total = jnp.sum(resid * resid, axis=0, keepdims=True)
        inverse_ref[r : r + 1, :] = 1.0 / (total + 1e-05)


def iterate(bounds_ref, high_ref, low_ref, inverse_ref, out_ref, res_ref, dir_ref, inc_ref):
    rows = 4
    members = LANES
    blocks = out_ref.shape[0] // rows
    lower = jnp.full((1, SPAN), bounds_ref[0], jnp.float32)
    higher = jnp.full((1, SPAN), bounds_ref[1], jnp.float32)
    theta = (higher + lower) / 2
    delta = (higher - lower) / 2
    sigma = theta / delta
    rho = 1.0 / sigma

    def product(value, r, axis):
        high = value.astype(jnp.bfloat16)
        low = (value - high.astype(jnp.float32)).astype(jnp.bfloat16)
        dims = (((1,), (axis,)), ((), ()))

        def dot(a, b):
            return lax.dot_general(a, b, dims, preferred_element_type=jnp.float32)

        both = dot(jnp.concatenate([high, low], axis=0), high_ref[r])
        return both[:members] + (both[members:] + dot(high, low_ref[r]))

    for r in range(rows):
        dir_ref[r] = res_ref[r] / theta
        inc_ref[r] = dir_ref[r]
    for _ in range(ITERS):
        rho_next = 1.0 / (2 * sigma - rho)
        for r in range(rows):
            direction = dir_ref[r]
            middle = product(direction, r, 0) * inverse_ref[r : r + 1, :]
            applied = product(middle, r, 1) + inverse_ref[4 + r : 5 + r, :] * direction
            residue = res_ref[r] - applied
            direction = (rho_next * rho) * direction + (2 * rho_next / delta) * residue
            res_ref[r] = residue
            dir_ref[r] = direction
            inc_ref[r] = inc_ref[r] + direction
        rho = rho_next
    for r in range(rows):
        out_ref[pl.ds(r, blocks, stride=rows), :] = inc_ref[r, :, :blocks].T


def vmem(count):
    return [pl.BlockSpec(memory_space=pltpu.VMEM)] * count


def hbm(count):
    return [pl.BlockSpec(memory_space=pltpu.HBM)] * count


def pack(pred_back, ridge, ensemble, observed, obs_var):
    local_blocks, rows, members = ensemble.shape
    peers = rows // 4
    operands = [
        pltpu.with_memory_space_constraint(value, pltpu.HBM)
        for value in (pred_back, ridge, ensemble, observed, obs_var)
    ]
    return pl.pallas_call(
        pack_kernel,
        out_shape=pltpu.VMEM((peers * CHUNK, members), jnp.float32),
        in_specs=hbm(5),
        out_specs=vmem(1)[0],
        scratch_shapes=[
            pltpu.SMEM(pred_back.shape, jnp.int32),
            pltpu.SMEM(ridge.shape, jnp.float32),
            pltpu.VMEM(ensemble.shape, jnp.float32),
            pltpu.VMEM(observed.shape, jnp.float32),
            pltpu.VMEM(obs_var.shape, jnp.float32),
            pltpu.SemaphoreType.DMA((6,)),
        ],
        compiler_params=PARAMS,
        name="pack",
    )(*operands)


def local(own):
    members = own.shape[1]
    flat = jax.ShapeDtypeStruct((4, members, LANES), jnp.float32)
    return pl.pallas_call(
        local_kernel,
        out_shape=[
            flat,
            flat,
            jax.ShapeDtypeStruct((8, LANES), jnp.float32),
            jax.ShapeDtypeStruct((REACH + 1, 4, LANES), jnp.float32),
        ],
        in_specs=vmem(1),
        out_specs=vmem(4),
        scratch_shapes=[pltpu.VMEM((2, 4 * LANES, members), jnp.float32)],
        compiler_params=PARAMS,
        name="local",
    )(own)


def solve(bounds, own, halo, mine):
    members, rows = own.shape[1], 4
    square = (rows, SPAN, SPAN)
    wide = pltpu.VMEM((rows, members, SPAN), jnp.float32)
    return pl.pallas_call(
        solve_kernel,
        out_shape=jax.ShapeDtypeStruct((own.shape[0] // CHUNK * 2 * rows, members), jnp.float32),
        in_specs=hbm(1) + vmem(8),
        out_specs=vmem(1)[0],
        scratch_shapes=[
            pltpu.VMEM((2, rows * LANES, members), jnp.float32),
            pltpu.VMEM((LANES, members), jnp.float32),
            wide,
            pltpu.VMEM(square, jnp.float32),
            pltpu.VMEM(square, jnp.bfloat16),
            pltpu.VMEM(square, jnp.bfloat16),
            pltpu.VMEM((8, SPAN), jnp.float32),
            pltpu.VMEM((REACH + 1, 8, LANES), jnp.float32),
            pltpu.VMEM((REACH, 8, LANES), jnp.float32),
            pltpu.VMEM((META, SPAN), jnp.float32),
            wide,
            wide,
            wide,
            pltpu.SMEM(bounds.shape, jnp.float32),
            pltpu.SemaphoreType.DMA,
        ],
        compiler_params=PARAMS,
        name="solve",
    )(pltpu.with_memory_space_constraint(bounds, pltpu.HBM), own, *halo[::-1], *mine)


def on_device(ensemble, observed, obs_var, ridge, pred_back, bounds):
    local_blocks, rows, members = ensemble.shape
    slots = pred_back.shape[1]
    region_blocks = lax.axis_size("blk") * local_blocks
    regions = lax.axis_size("region")
    per_device = rows // lax.axis_size("blk")
    assert (local_blocks, per_device, members, region_blocks) == (2, 4, LANES, LANES)
    groups = rows // 8
    peers = 2 * groups
    odd = (lax.axis_index("blk") & 1).astype(jnp.uint32)
    edge = HALO // local_blocks
    start = (1 - odd) * (peers - edge)
    observed, start = lax.optimization_barrier((observed, start))
    packed = pack(pred_back, ridge, ensemble, observed, obs_var)
    own = lax.all_to_all(packed.reshape(peers, 1, CHUNK * members), "blk", 0, 0, tiled=True)
    flat = own.reshape(peers * CHUNK, members)
    mine = local(flat)

    def pairs(core, step):
        return [
            (region * peers + place, (region + step) * peers + place)
            for region in range(regions)
            for place in range(core, peers, 2)
            if 0 <= region + step < regions
        ]

    none = jnp.uint32(0)
    middle = lax.dynamic_slice(own, (start, none, none), (edge, 1, own.shape[2]))
    first = lax.ppermute(own[:edge], AXES, pairs(0, -1))
    second = lax.ppermute(middle, AXES, pairs(1, -1) + pairs(0, 1))
    third = lax.ppermute(own[peers - edge :], AXES, pairs(1, 1))
    halo = [part.reshape(edge * CHUNK, members) for part in (first, second, third)]
    increment = solve(bounds, flat, halo, mine)
    increment = increment.reshape(2 * groups, local_blocks * per_device, members)
    increment = lax.all_to_all(increment, "blk", 0, 0, tiled=True)
    return pl.pallas_call(
        add_kernel,
        out_shape=jax.ShapeDtypeStruct(ensemble.shape, jnp.float32),
        in_specs=vmem(2),
        out_specs=vmem(1)[0],
        compiler_params=PARAMS,
        name="add",
    )(ensemble, increment.reshape(groups, 2, 8, members))


def solution(mesh):
    return jax.shard_map(
        on_device,
        mesh=mesh,
        in_specs=(
            P(AXES, None, None),
            P(AXES, None, None),
            P(AXES, None),
            P(AXES),
            P(AXES, None),
            P(),
        ),
        out_specs=P(AXES, None, None),
        check_vma=False,
    )
```
